256 devices in a mesh: tm: 64 (over y_hi, z, x), head: 4 (over y_lo, core).
Axes of the slice: x: 4, y: 4 (y_hi: 2, y_lo: 2; y = y_hi * 2 + y_lo), z: 8, core: 2. Of those that a mesh axis runs over, the one named last changes fastest.
Arguments:
- query: bfloat16 [32768, 2560], P(('tm', 'head')), may hold values from -5 to 5, as said below
- keys: bfloat16 [32768, 2560], P(('tm', 'head')), may hold values from -5 to 5, as said below
- values: bfloat16 [32768, 2560], P(('tm', 'head')), may hold values from -6 to 6
- grad_out: bfloat16 [32768, 2560], P(('tm', 'head')), may hold values from -6 to 6
- tile_pattern: int32 [3, 4, 3], replicated, may hold values from 0 to 3, as said below
- window: int32 [64], replicated, may hold values from 1 to 3
Outputs:
- attended: bfloat16 [32768, 2560], P(('tm', 'head'))
- grad_query: bfloat16 [32768, 2560], P(('tm', 'head'))
- grad_keys: bfloat16 [32768, 2560], P(('tm', 'head'))
- grad_values: bfloat16 [32768, 2560], P(('tm', 'head'))
The draws below stay inside these ranges and needn't reach their ends.
Inputs may be any that keep to these rules, and one draw needn't show every extreme that they name: `query`: queries of the attention. `keys`: keys of the attention. `tile_pattern`: entry [l, q, 0] is q; the 3 entries of each row are distinct.
All inputs are finite; a program needn't handle non-finite values.
Results may differ from the reference program's by a relative error of at most 0.0091.
Values may be sent and summed in bfloat16 or wider, within the bound.
A program may use at most 128 MiB of HBM per device.

```python
import math
import jax
import jax.numpy as jnp
from jax import lax

HD = 128
TILE = 128
QT = 4
SEL = 3
W = 3
FRAMES = 64
HEADS = 20
TOKENS = 32768
DA = 2560


def drawn_pair(key):
    base = jax.random.fold_in(key, 7)
    first, second = jax.random.split(base, 2)
    shape = (TOKENS, HEADS * HD)
    query = jnp.clip(jax.random.normal(first, shape, jnp.float32), -5.0, 5.0)
    keyset = jnp.clip(jax.random.normal(second, shape, jnp.float32), -5.0, 5.0)
    return (query, keyset)


def draw_query(key, part):
    return drawn_pair(key)[0].astype(jnp.bfloat16)


def draw_keys(key, part):
    return drawn_pair(key)[1].astype(jnp.bfloat16)


def draw_tile_pattern(key, part):
    base = jax.random.fold_in(key, 13)
    row_keys = jax.random.split(base, W * QT)
    others = jax.vmap(lambda row_key: jax.random.permutation(row_key, QT - 1)[:SEL - 1])(row_keys)
    others = others.reshape(W, QT, SEL - 1)
    own = jnp.broadcast_to(jnp.arange(QT, dtype=jnp.int32)[None, :, None], (W, QT, 1))
    picked = (own + 1 + others) % QT
    return jnp.concatenate([own, picked], -1).astype(jnp.int32)


def draw_window(key, part):
    base = jax.random.fold_in(key, 11)
    first, second = jax.random.split(base, 2)
    widths = jax.random.randint(first, (FRAMES,), 1, W + 1)
    spots = jax.random.permutation(second, FRAMES)
    widths = widths.at[spots[0]].set(W).at[spots[1]].set(1)
    return widths.astype(jnp.int32)


def levels(own_key, extent, cuts, low, largest):
    level = 1.0
    for dim, blocks in cuts:
        steps = jax.random.uniform(jax.random.fold_in(jax.random.fold_in(own_key, 6), dim), (blocks,), jnp.float32, low / len(cuts), largest / len(cuts))
        level = level * jnp.repeat(jnp.exp(steps), extent[dim] // blocks).reshape((-1,) + (1,) * (len(extent) - 1 - dim))
    return level


def scatter_about(rng, dims, scale, most, cuts=(), kind=jnp.bfloat16):
    level = levels(rng, dims, cuts, -0.22, 0.18) if cuts else 1.0
    values = jax.random.normal(rng, dims, jnp.float32) * scale * level
    return jnp.minimum(jnp.maximum(values, -most), most).astype(kind)


def setup_inputs(seed: int = 0) -> dict:
    arg_keys = jax.random.split(jax.random.key(seed), 7)
    query = draw_query(jax.random.fold_in(arg_keys[6], 71), 0)
    keys = draw_keys(jax.random.fold_in(arg_keys[6], 71), 0)
    values = scatter_about(arg_keys[2], (TOKENS, DA), 1.0, 6.0, ((0, 256),))
    grad_out = scatter_about(arg_keys[3], (TOKENS, DA), 1.0, 6.0, ((0, 256),))
    tile_pattern = draw_tile_pattern(jax.random.fold_in(arg_keys[6], 71), 0)
    window = draw_window(jax.random.fold_in(arg_keys[6], 71), 0)
    return {"query": query, "keys": keys, "values": values, "grad_out": grad_out, "tile_pattern": tile_pattern, "window": window}


NEG = -1e+30

def frame_pass(q_head, k_head, v_head, g_head, tile_pattern, window, frame):
    scale = 1.0 / math.sqrt(HD)
    highest = lax.Precision.HIGHEST
    query = lax.dynamic_index_in_dim(q_head, frame, 0, False).astype(jnp.float32)
    grad = lax.dynamic_index_in_dim(g_head, frame, 0, False).astype(jnp.float32)
    key_parts = []
    val_parts = []
    for lag in range(W):
        source = jnp.maximum(frame - lag, 0).astype(jnp.int32)
        key_frame = lax.dynamic_index_in_dim(k_head, source, 0, False)
        val_frame = lax.dynamic_index_in_dim(v_head, source, 0, False)
        key_parts.append(jnp.take(key_frame, tile_pattern[lag], axis=0))
        val_parts.append(jnp.take(val_frame, tile_pattern[lag], axis=0))
    count = W * SEL * TILE
    keyset = jnp.stack(key_parts, 1).reshape(QT, count, HD).astype(jnp.float32)
    valset = jnp.stack(val_parts, 1).reshape(QT, count, HD).astype(jnp.float32)
    lags = jnp.arange(W, dtype=jnp.int32)
    limit = window[frame]
    live = (lags <= frame) & (lags < limit)
    live_cols = jnp.repeat(live, SEL * TILE)
    scores = jnp.einsum('qad,qbd->qab', query, keyset) * scale
    scores = jnp.where(live_cols, scores, NEG)
    top = lax.optimization_barrier(jnp.max(scores, -1, keepdims=True))
    expo = jnp.exp(scores - top)
    prob = expo / lax.optimization_barrier(jnp.sum(expo, -1, keepdims=True))
    prob_b = lax.optimization_barrier(prob.astype(jnp.bfloat16)).astype(jnp.float32)
    output = jnp.einsum('qab,qbd->qad', prob_b, valset)
    delta = lax.optimization_barrier(jnp.sum(grad * output, -1, keepdims=True))
    dprob = jnp.einsum('qad,qbd->qab', grad, valset)
    dscore = lax.optimization_barrier((prob * (dprob - delta) * scale).astype(jnp.bfloat16)).astype(jnp.float32)
    dquery = jnp.einsum('qab,qbd->qad', dscore, keyset)
    dkeys = jnp.einsum('qab,qad->qbd', dscore, query).reshape(QT, W, SEL, TILE, HD)
    dvals = jnp.einsum('qab,qad->qbd', prob_b, grad).reshape(QT, W, SEL, TILE, HD)
    onehot = (tile_pattern[:, :, :, None] == jnp.arange(QT, dtype=jnp.int32)).astype(jnp.float32)
    spread_k = jnp.einsum('qwstd,wqsk->wktd', dkeys, onehot, precision=highest)
    spread_v = jnp.einsum('qwstd,wqsk->wktd', dvals, onehot, precision=highest)
    return (output.astype(jnp.bfloat16), dquery.astype(jnp.bfloat16), spread_k[0], spread_v[0], spread_k[1:], spread_v[1:])

def shift_up(array):
    padding = jnp.zeros((1,) + array.shape[1:], jnp.float32)
    return jnp.concatenate([array[1:], padding], 0)

def round_trip(array):
    return lax.optimization_barrier(array.astype(jnp.bfloat16)).astype(jnp.float32)

def head_pass(q_head, k_head, v_head, g_head, tile_pattern, window):
    frames = jnp.arange(FRAMES, dtype=jnp.int32)
    results = lax.map(lambda frame: frame_pass(q_head, k_head, v_head, g_head, tile_pattern, window, frame), frames)
    output, dquery, own_k, own_v, far_k, far_v = results
    pending_k = round_trip(far_k[:, W - 2])
    pending_v = round_trip(far_v[:, W - 2])
    for lag in range(W - 1, 0, -1):
        moved_k = shift_up(pending_k)
        moved_v = shift_up(pending_v)
        if lag > 1:
            pending_k = round_trip(far_k[:, lag - 2] + moved_k)
            pending_v = round_trip(far_v[:, lag - 2] + moved_v)
        else:
            pending_k = moved_k
            pending_v = moved_v
    total_k = own_k + pending_k
    total_v = own_v + pending_v
    return (output, dquery, total_k.astype(jnp.bfloat16), total_v.astype(jnp.bfloat16))

def split_heads(array):
    return jnp.transpose(array.reshape(FRAMES, QT, TILE, HEADS, HD), (3, 0, 1, 2, 4))

def join_heads(array):
    return jnp.transpose(array, (1, 2, 3, 0, 4)).reshape(TOKENS, HEADS * HD)

def reference(query, keys, values, grad_out, tile_pattern, window):
    groups = (split_heads(query), split_heads(keys), split_heads(values), split_heads(grad_out))
    results = lax.map(lambda group: head_pass(group[0], group[1], group[2], group[3], tile_pattern, window), groups)
    return (join_heads(results[0]), join_heads(results[1]), join_heads(results[2]), join_heads(results[3]))
```

```python
import functools
import math

import jax
import jax.numpy as jnp
from jax import lax
from jax.experimental import pallas as pl
from jax.experimental.pallas import tpu as pltpu
from jax.sharding import PartitionSpec as P

HD = 128
TILE = 128
QT = 4
SEL = 3
W = 3
QH = 2
QB = QT // QH * TILE
NEG = -1e30
SCALE = 1.0 / math.sqrt(HD)
LOG2E = 1.0 / math.log(2.0)
MESH = pl.DeviceIdType.MESH
BF = jnp.bfloat16
F32 = jnp.float32


def kernel(
    n, heads,
    pat_ref, win_ref, q_ref, k_ref, v_ref, g_ref,
    o_ref, dq_ref, dk_ref, dv_ref,
    qg, kv, bias, kt, vt, score, pt, dst, keep0, keep1,
    a_out, a_in, b_out, b_in, outb,
    in_send, kv_in, qg_in, own_send, lag1_in, fwd_send, lag2_in,
    a_send, a_recv, b_send, b_recv, out_send, out_recv,
):
    f = lax.axis_index("tm")
    j = lax.axis_index("head")
    half = n // 2

    def group_of(seat):
        return lax.rem(seat + 2 * (f // half), QT)

    nxt = (f + 1, lax.rem(j + 2 * ((f + 1) // half - f // half), QT))
    prv = (f - 1, lax.rem(j + 2 * (f // half - (f + half - 1) // half + 1), QT))

    barrier = pltpu.get_barrier_semaphore()
    for d in range(1, QT):
        pl.semaphore_signal(barrier, inc=1, device_id=(f, lax.rem(j + d, QT)), device_id_type=MESH)

    @pl.when(f < n - 1)
    def _():
        pl.semaphore_signal(barrier, inc=1, device_id=nxt, device_id_type=MESH)

    @pl.when(f > 0)
    def _():
        pl.semaphore_signal(barrier, inc=1, device_id=prv, device_id_type=MESH)

    pl.semaphore_wait(barrier, QT - 1 + (f + n - 1) // n + (2 * n - 2 - f) // n)

    def columns(group, i):
        return pl.ds(pl.multiple_of((group * heads + i) * HD, HD), HD)

    def wait_for(ref, sem):
        pltpu.make_async_copy(ref, ref, sem).wait()

    def send(src, dst, ssem, rsem, device):
        pltpu.make_async_remote_copy(
            src_ref=src, dst_ref=dst, send_sem=ssem, recv_sem=rsem,
            device_id=device, device_id_type=MESH,
        ).start()

    def enter(i, refs, slot, sem):
        for d in range(1, QT):
            seat = lax.rem(j + d, QT)
            for a, ref in enumerate(refs):
                send(ref.at[:, columns(group_of(seat), i)], slot.at[a, j],
                     in_send.at[i], sem, (f, seat))
        for a, ref in enumerate(refs):
            pltpu.make_async_copy(ref.at[:, columns(group_of(j), i)], slot.at[a, j], sem).start()

    @pl.loop(0, heads)
    def _(i):
        enter(i, (k_ref, v_ref), kv.at[i, 0], kv_in.at[i])

        @pl.when(f < n - 1)
        def _():
            for a, ref in enumerate((k_ref, v_ref)):
                send(ref.at[:, columns(group_of(j), i)], kv.at[i, 1, a, j],
                     own_send.at[i], lag1_in.at[i], nxt)

        enter(i, (q_ref, g_ref), qg.at[i], qg_in.at[i])

    lane = lax.broadcasted_iota(jnp.int32, (1, QB), 1)
    limit = win_ref[f]
    for h in range(QH):
        for lag in range(W):
            for t in range(QT):
                pair = []
                for tile in (2 * h, 2 * h + 1):
                    hit = pat_ref[lag, tile, 0] == t
                    for s in range(1, SEL):
                        hit = hit | (pat_ref[lag, tile, s] == t)
                    hit = hit & (lag <= f) & (lag < limit)
                    pair.append(jnp.where(hit, 0.0, NEG).astype(F32))
                bias[h, lag * QT + t] = jnp.where(lane < TILE, pair[0], pair[1])

    @pl.when(f == 0)
    def _():
        @pl.loop(0, heads)
        def _(i):
            kv[i, 1] = jnp.zeros(kv.shape[2:], BF)
            kv[i, 2] = jnp.zeros(kv.shape[2:], BF)

    @pl.when(f == n - 1)
    def _():
        @pl.loop(0, heads)
        def _(i):
            a_in[i] = jnp.zeros(a_in.shape[1:], BF)
            b_in[i] = jnp.zeros(b_in.shape[1:], BF)

    def own(i):
        wait_for(kv.at[i, 0], kv_in.at[i])

        @pl.when(f < n - 1)
        def _():
            for d in range(1, QT):
                t = lax.rem(j + d, QT)
                for a in range(2):
                    send(kv.at[i, 0, a, t], kv.at[i, 1, a, t], own_send.at[i], lag1_in.at[i], nxt)

    def forward(i):
        @pl.when(f > 0)
        def _():
            wait_for(kv.at[i, 1], lag1_in.at[i])

        @pl.when(f < n - 1)
        def _():
            send(kv.at[i, 1], kv.at[i, 2], fwd_send.at[i], lag2_in.at[i], nxt)

    def leave(i, a):
        outs = (o_ref, dq_ref, dk_ref, dv_ref)
        where_to = outs[a].at[:, columns(group_of(j), i)]
        for d in range(1, QT):
            seat = lax.rem(j + d, QT)
            send(outb.at[i, a, seat], where_to, out_send.at[i], out_recv.at[a], (f, seat))
        pltpu.make_async_copy(outb.at[i, a, j], where_to, out_recv.at[a]).start()

    def flat(ref):
        return ref[...].reshape(QT * TILE, HD)

    def attend(i):
        for lag in range(W):
            kt[lag] = flat(kv.at[i, lag, 0]).T
            vt[lag] = flat(kv.at[i, lag, 1]).T

        @pl.loop(0, QH)
        def _(h):
            two = pl.ds(2 * h, 2)
            qh = qg[i, 0, two].reshape(QB, HD)
            gh = qg[i, 1, two].reshape(QB, HD)
            top = None
            for lag in range(W):
                for t in range(QT):
                    r = lag * QT + t
                    s = lax.dot_general(kv[i, lag, 0, t], qh, (((1,), (1,)), ((), ())),
                                        preferred_element_type=F32)
                    score[r] = s
                    here = jnp.max(s, axis=0, keepdims=True) + bias[h, r]
                    top = here if top is None else jnp.maximum(top, here)
            factor = SCALE * LOG2E
            total = jnp.zeros((1, QB), F32)
            for r in range(W * QT):
                e = jnp.exp2(score[r] * factor + (bias[h, r] - top) * factor)
                score[r] = e
                total = total + jnp.sum(e, axis=0, keepdims=True)
            inverse = 1.0 / total
            for r in range(W * QT):
                pt[h, r] = (score[r] * inverse).astype(BF)
            out = jnp.zeros((HD, QB), F32)
            for lag in range(W):
                probs = pt[h, lag * QT:(lag + 1) * QT].reshape(QT * TILE, QB)
                out = out + jnp.dot(vt[lag], probs, preferred_element_type=F32)
            delta = jnp.sum(gh.T.astype(F32) * out, axis=0, keepdims=True)
            outb[i, 0, two] = out.astype(BF).T.reshape(2, TILE, HD)
            scaled = inverse * SCALE
            for lag in range(W):
                for t in range(QT):
                    r = lag * QT + t
                    dp = lax.dot_general(kv[i, lag, 1, t], gh, (((1,), (1,)), ((), ())),
                                         preferred_element_type=F32)
                    dst[h, r] = (score[r] * scaled * (dp - delta)).astype(BF)
            dq = jnp.zeros((HD, QB), F32)
            for lag in range(W):
                ds = dst[h, lag * QT:(lag + 1) * QT].reshape(QT * TILE, QB)
                dq = dq + jnp.dot(kt[lag], ds, preferred_element_type=F32)
            outb[i, 1, two] = dq.astype(BF).T.reshape(2, TILE, HD)

        for lag in range(W):
            for a, (grads, rows) in enumerate(((dst, qg.at[i, 0]), (pt, qg.at[i, 1]))):
                acc = jnp.zeros((QT * TILE, HD), F32)
                for h in range(QH):
                    block = grads[h, lag * QT:(lag + 1) * QT].reshape(QT * TILE, QB)
                    acc = acc + jnp.dot(block, rows[2 * h:2 * h + 2].reshape(QB, HD),
                                        preferred_element_type=F32)
                acc = acc.reshape(QT, TILE, HD)
                if lag == 0:
                    keep0[i, a] = acc
                elif lag == 1:
                    keep1[i, a] = acc
                else:
                    a_out[i, a] = acc.astype(BF)

    def compute(i):
        wait_for(qg.at[i], qg_in.at[i])

        @pl.when(f > 0)
        def _():
            wait_for(kv.at[i, 2], lag2_in.at[i])

        attend(i)

        @pl.when(f > 0)
        def _():
            for a in range(2):
                send(a_out.at[i, a], a_in.at[i, a], a_send.at[i, a], a_recv.at[i, a], prv)

        leave(i, 0)
        leave(i, 1)

    def chain(i):
        for a in range(2):
            @pl.when(f < n - 1)
            def _():
                wait_for(a_in.at[i, a], a_recv.at[i, a])

            b_out[i, a] = (keep1[i, a] + a_in[i, a].astype(F32)).astype(BF)

            @pl.when(f > 0)
            def _():
                send(b_out.at[i, a], b_in.at[i, a], b_send.at[i, a], b_recv.at[i, a], prv)

    def finish(i):
        for a in range(2):
            @pl.when(f < n - 1)
            def _():
                wait_for(b_in.at[i, a], b_recv.at[i, a])

            outb[i, 2 + a] = (keep0[i, a] + b_in[i, a].astype(F32)).astype(BF)
            leave(i, 2 + a)

    own(0)

    @pl.loop(0, heads + 3)
    def _(s):
        @pl.when(s + 1 < heads)
        def _():
            own(s + 1)

        @pl.when(s < heads)
        def _():
            forward(s)

        @pl.when((s >= 1) & (s < heads + 1))
        def _():
            compute(s - 1)

        @pl.when((s >= 2) & (s < heads + 2))
        def _():
            chain(s - 2)

        @pl.when(s >= 3)
        def _():
            finish(s - 3)

    @pl.loop(0, heads)
    def _(i):
        wait_for(outb.at[i, 0:3], in_send.at[i])
        wait_for(outb.at[i, 0:3], out_send.at[i])

        @pl.when(f < n - 1)
        def _():
            wait_for(kv.at[i, 0], own_send.at[i])
            wait_for(kv.at[i, 1], fwd_send.at[i])

        @pl.when(f > 0)
        def _():
            for a in range(2):
                wait_for(a_out.at[i, a], a_send.at[i, a])
                wait_for(b_out.at[i, a], b_send.at[i, a])

    for a, ref in enumerate((o_ref, dq_ref, dk_ref, dv_ref)):
        wait_for(ref, out_recv.at[a])


def shards(n, query, keys, values, grad_out, tile_pattern, window):
    rows, width = query.shape
    heads = width // HD // QT
    blocks = (QT, TILE, HD)
    dma = pltpu.SemaphoreType.DMA
    scratch = [
        pltpu.VMEM((heads, 2) + blocks, BF),
        pltpu.VMEM((heads, W, 2) + blocks, BF),
        pltpu.VMEM((QH, W * QT, 1, QB), F32),
        pltpu.VMEM((W, HD, QT * TILE), BF),
        pltpu.VMEM((W, HD, QT * TILE), BF),
        pltpu.VMEM((W * QT, TILE, QB), F32),
        pltpu.VMEM((QH, W * QT, TILE, QB), BF),
        pltpu.VMEM((QH, W * QT, TILE, QB), BF),
        pltpu.VMEM((heads, 2) + blocks, F32),
        pltpu.VMEM((heads, 2) + blocks, F32),
        pltpu.VMEM((heads, 2) + blocks, BF),
        pltpu.VMEM((heads, 2) + blocks, BF),
        pltpu.VMEM((heads, 2) + blocks, BF),
        pltpu.VMEM((heads, 2) + blocks, BF),
        pltpu.VMEM((heads, 4) + blocks, BF),
        dma((heads,)), dma((heads,)), dma((heads,)),
        dma((heads,)), dma((heads,)), dma((heads,)), dma((heads,)),
        dma((heads, 2)), dma((heads, 2)), dma((heads, 2)), dma((heads, 2)),
        dma((heads,)), dma((4,)),
    ]
    smem = pl.BlockSpec(memory_space=pltpu.SMEM)
    anywhere = pl.BlockSpec(memory_space=pl.ANY)
    return pl.pallas_call(
        functools.partial(kernel, n, heads),
        out_shape=[jax.ShapeDtypeStruct((rows, width), BF)] * 4,
        in_specs=[smem, smem] + [anywhere] * 4,
        out_specs=[anywhere] * 4,
        scratch_shapes=scratch,
        compiler_params=pltpu.CompilerParams(
            collective_id=0, has_side_effects=True, vmem_limit_bytes=56 * 1024 * 1024
        ),
    )(tile_pattern, window, query, keys, values, grad_out)


def solution(mesh):
    rows = P(("tm", "head"), None)
    return jax.shard_map(
        functools.partial(shards, mesh.shape["tm"]),
        mesh=mesh,
        in_specs=(rows, rows, rows, rows, P(), P()),
        out_specs=(rows, rows, rows, rows),
        check_vma=False,
    )
```

```python
import functools
import math

import jax
import jax.numpy as jnp
from jax import lax
from jax.experimental import pallas as pl
from jax.experimental.pallas import tpu as pltpu
from jax.sharding import PartitionSpec as P

HD = 128
TILE = 128
QT = 4
SEL = 3
W = 3
QH = 2
QB = QT // QH * TILE
NEG = -1e30
SCALE = 1.0 / math.sqrt(HD)
FACTOR = SCALE / math.log(2.0)
MESH = pl.DeviceIdType.MESH
BF = jnp.bfloat16
F32 = jnp.float32


def kernel(
    n, chip_heads,
    pat_ref, win_ref, q_ref, k_ref, v_ref, g_ref,
    o_ref, dq_ref, dk_ref, dv_ref,
    qg, kv, bias, kt, vt, score, pt, dst, gs, acc, g_out, g_in, outb,
    in_send, kv_in, qg_in, next_send, next_in, g_send, g_recv, out_send, out_recv,
):
    f = lax.axis_index("tm")
    seat = lax.axis_index("head")
    half = n // 2
    pair, side = f // 2, lax.rem(f, 2)
    pairs = n // 2
    most = (chip_heads + 1) // 2

    def count(at):
        return (chip_heads + 1 - lax.rem(at, 2)) // 2

    def first_head(other, at):
        row = lax.rem(other + pair, 2)
        column = lax.rem(at // 2 + f // half, 2)
        return (row * 2 + column) * chip_heads + lax.rem(at, 2) * most

    def linked(step):
        frame = 2 * (pair + step) + 1 - side
        turn = (frame + n) // half - (f + n) // half
        return (frame, lax.rem(seat + 2 * turn + 2 * QT, QT))

    nxt, prv = linked(1), linked(-1)
    has_next = pair < pairs - 1
    has_prev = pair > 0
    mine = count(seat)
    peers = [(dx, dj) for dj in range(QT) for dx in (1, 0)]

    def peer(dx, dj):
        return lax.rem(side + dx, 2), lax.rem(seat + dj, QT)

    barrier = pltpu.get_barrier_semaphore()
    for dx, dj in peers:
        if dx or dj:
            other, at = peer(dx, dj)
            pl.semaphore_signal(barrier, inc=1, device_id=(2 * pair + other, at), device_id_type=MESH)

    @pl.when(has_next)
    def _():
        pl.semaphore_signal(barrier, inc=1, device_id=nxt, device_id_type=MESH)

    @pl.when(has_prev)
    def _():
        pl.semaphore_signal(barrier, inc=1, device_id=prv, device_id_type=MESH)

    pl.semaphore_wait(barrier, 2 * QT - 1 + (pair + pairs - 1) // pairs + (2 * pairs - 2 - pair) // pairs)

    def columns(head):
        return pl.ds(pl.multiple_of(head * HD, HD), HD)

    def wait_for(ref, sem):
        pltpu.make_async_copy(ref, ref, sem).wait()

    def send(src, dst, ssem, rsem, device):
        pltpu.make_async_remote_copy(
            src_ref=src, dst_ref=dst, send_sem=ssem, recv_sem=rsem,
            device_id=device, device_id_type=MESH,
        ).start()

    def enter(i, refs, slot, sem):
        for dx, dj in peers:
            other, at = peer(dx, dj)
            cols = columns(first_head(other, at) + i)

            @pl.when(i < count(at))
            def _():
                for a, ref in enumerate(refs):
                    if dx or dj:
                        send(ref.at[:, cols], slot.at[a, seat], in_send.at[i, 2 * dj + dx], sem,
                             (2 * pair + other, at))
                    else:
                        pltpu.make_async_copy(ref.at[:, cols], slot.at[a, seat], sem).start()

    @pl.loop(0, most)
    def _(i):
        enter(i, (k_ref, v_ref), kv.at[i, 1 - side], kv_in.at[i])
        enter(i, (q_ref, g_ref), qg.at[i, side], qg_in.at[i])

    lane = lax.broadcasted_iota(jnp.int32, (1, QB), 1)
    for x in range(2):
        frame = 2 * pair + x
        limit = win_ref[frame]
        for h in range(QH):
            for lag in range(W):
                for t in range(QT):
                    both = []
                    for tile in (2 * h, 2 * h + 1):
                        hit = pat_ref[lag, tile, 0] == t
                        for s in range(1, SEL):
                            hit = hit | (pat_ref[lag, tile, s] == t)
                        hit = hit & (lag <= frame) & (lag < limit)
                        both.append(jnp.where(hit, 0.0, NEG).astype(F32))
                    bias[x, h, lag * QT + t] = jnp.where(lane < TILE, both[0], both[1])

    @pl.loop(0, most)
    def _(i):
        acc[i] = jnp.zeros(acc.shape[1:], F32)

        @pl.when(pair == 0)
        def _():
            kv[i, 2] = jnp.zeros(kv.shape[2:], BF)
            kv[i, 3] = jnp.zeros(kv.shape[2:], BF)

        @pl.when(pair == pairs - 1)
        def _():
            g_in[i] = jnp.zeros(g_in.shape[1:], BF)

    def own(i):
        wait_for(kv.at[i, 0:2], kv_in.at[i])

        @pl.when(has_next)
        def _():
            for s in range(2):
                send(kv.at[i, s], kv.at[i, 2 + s], next_send.at[i, s], next_in.at[i, s], nxt)

    def leave(i, x, a):
        ref = (o_ref, dq_ref, dk_ref, dv_ref)[a]
        where_to = ref.at[:, columns(first_head(side, seat) + i)]
        for dj in range(QT):
            at = lax.rem(seat + dj, QT)
            if dj:
                send(outb.at[i, x, a, at], where_to, out_send.at[i, x, a, dj], out_recv.at[a],
                     (2 * pair + x, at))
            else:
                @pl.when(x == side)
                def _():
                    pltpu.make_async_copy(outb.at[i, x, a, at], where_to, out_recv.at[a]).start()

                @pl.when(x != side)
                def _():
                    send(outb.at[i, x, a, at], where_to, out_send.at[i, x, a, dj], out_recv.at[a],
                         (2 * pair + 1 - side, at))

    def nt(a, b):
        return lax.dot_general(a, b, (((1,), (1,)), ((), ())), preferred_element_type=F32)

    def mm(a, b):
        return jnp.dot(a, b, preferred_element_type=F32)

    def fold(block, op):
        return op(block.reshape(TILE // 8, 8, QB), axis=0)

    def attend(i, x):
        base = 1 - x

        def turn(slot):
            kt[slot] = kv[i, slot, 0].reshape(QT * TILE, HD).T
            vt[slot] = kv[i, slot, 1].reshape(QT * TILE, HD).T

        @pl.when(x == 1)
        def _():
            for slot in range(3):
                turn(slot)

        @pl.when(x == 0)
        def _():
            turn(3)

        for h in range(QH):
            lanes = slice(h * QB, (h + 1) * QB)
            qh = qg[i, x, 0, 2 * h:2 * h + 2].reshape(QB, HD)
            gh = qg[i, x, 1, 2 * h:2 * h + 2].reshape(QB, HD)
            top = None
            for lag in range(W):
                for t in range(QT):
                    r = lag * QT + t
                    s = nt(kv[i, base + lag, 0, t], qh)
                    score[h, r] = s
                    here = fold(s, jnp.max) + bias[x, h, r]
                    top = here if top is None else jnp.maximum(top, here)
            top = jnp.max(top, axis=0, keepdims=True)
            total = None
            for r in range(W * QT):
                e = jnp.exp2(score[h, r] * FACTOR + (bias[x, h, r] - top) * FACTOR)
                pt[r, :, lanes] = e.astype(BF)
                here = fold(e, jnp.sum)
                total = here if total is None else total + here
            inverse = 1.0 / jnp.sum(total, axis=0, keepdims=True)
            out = None
            for lag in range(W):
                probs = pt[lag * QT:(lag + 1) * QT, :, lanes].reshape(QT * TILE, QB)
                here = mm(vt[base + lag], probs)
                out = here if out is None else out + here
            out = out * inverse
            scaled = (gh.T.astype(F32) * inverse).astype(BF)
            delta = jnp.sum(scaled.astype(F32) * out, axis=0, keepdims=True)
            outb[i, x, 0, 2 * h:2 * h + 2] = out.astype(BF).T.reshape(2, TILE, HD)
            back = scaled.T
            gs[lanes] = back
            for lag in range(W):
                for t in range(QT):
                    r = lag * QT + t
                    dp = nt(kv[i, base + lag, 1, t], back) - delta
                    dst[r, :, lanes] = dp.astype(BF) * pt[r, :, lanes]
            dq = None
            for lag in range(W):
                ds = dst[lag * QT:(lag + 1) * QT, :, lanes].reshape(QT * TILE, QB)
                here = mm(kt[base + lag], ds)
                dq = here if dq is None else dq + here
            outb[i, x, 1, 2 * h:2 * h + 2] = (dq * SCALE).astype(BF).T.reshape(2, TILE, HD)

        rows = qg[i, x, 0].reshape(QT * TILE, HD)
        for lag in range(W):
            block = dst[lag * QT:(lag + 1) * QT].reshape(QT * TILE, QT * TILE)
            acc[i, base + lag, 0] += (mm(block, rows) * SCALE).reshape(QT, TILE, HD)
            block = pt[lag * QT:(lag + 1) * QT].reshape(QT * TILE, QT * TILE)
            acc[i, base + lag, 1] += mm(block, gs[...]).reshape(QT, TILE, HD)

    def finish(i):
        for s in range(2):
            for a in range(2):
                @pl.when(has_next)
                def _():
                    wait_for(g_in.at[i, s, a], g_recv.at[i, s, a])

                outb[i, 1 - s, 2 + a] = (acc[i, s, a] + g_in[i, s, a].astype(F32)).astype(BF)
                leave(i, 1 - s, 2 + a)

    own(0)

    @pl.loop(0, 2 * most + 2)
    def _(u):
        i, odd = u // 2, lax.rem(u, 2)

        @pl.when(i < mine)
        def _():
            @pl.when(odd == 0)
            def _():
                wait_for(qg.at[i], qg_in.at[i])

            @pl.when(has_prev)
            def _():
                wait_for(kv.at[i, 2 + odd], next_in.at[i, odd])

            attend(i, 1 - odd)
            leave(i, 1 - odd, 0)
            leave(i, 1 - odd, 1)

            @pl.when((odd == 1) & has_prev)
            def _():
                for s in range(2):
                    for a in range(2):
                        g_out[i, s, a] = acc[i, 2 + s, a].astype(BF)
                        send(g_out.at[i, s, a], g_in.at[i, s, a], g_send.at[i, s, a],
                             g_recv.at[i, s, a], prv)

        @pl.when((odd == 0) & (i + 1 < mine))
        def _():
            own(i + 1)

        @pl.when((odd == 1) & (i >= 1) & (i < mine + 1))
        def _():
            finish(i - 1)

    @pl.loop(0, most)
    def _(i):
        for dx, dj in peers:
            if dx or dj:
                @pl.when(i < count(peer(dx, dj)[1]))
                def _():
                    wait_for(qg.at[i, 0, 0], in_send.at[i, 2 * dj + dx])

        @pl.when(i < mine)
        def _():
            for x in range(2):
                for a in range(4):
                    for dj in range(QT):
                        if dj:
                            wait_for(outb.at[i, x, a, dj], out_send.at[i, x, a, dj])
                        else:
                            @pl.when(x != side)
                            def _():
                                wait_for(outb.at[i, x, a, dj], out_send.at[i, x, a, dj])

            for s in range(2):
                @pl.when(has_next)
                def _():
                    wait_for(kv.at[i, s], next_send.at[i, s])

                @pl.when(has_prev)
                def _():
                    for a in range(2):
                        wait_for(g_out.at[i, s, a], g_send.at[i, s, a])

    for a, ref in enumerate((o_ref, dq_ref, dk_ref, dv_ref)):
        wait_for(ref, out_recv.at[a])


def shards(n, query, keys, values, grad_out, tile_pattern, window):
    rows, width = query.shape
    chip_heads = width // HD // 4
    most = (chip_heads + 1) // 2
    blocks = (QT, TILE, HD)
    dma = pltpu.SemaphoreType.DMA
    scratch = [
        pltpu.VMEM((most, 2, 2) + blocks, BF),
        pltpu.VMEM((most, 4, 2) + blocks, BF),
        pltpu.VMEM((2, QH, W * QT, 1, QB), F32),
        pltpu.VMEM((4, HD, QT * TILE), BF),
        pltpu.VMEM((4, HD, QT * TILE), BF),
        pltpu.VMEM((QH, W * QT, TILE, QB), F32),
        pltpu.VMEM((W * QT, TILE, QT * TILE), BF),
        pltpu.VMEM((W * QT, TILE, QT * TILE), BF),
        pltpu.VMEM((QT * TILE, HD), BF),
        pltpu.VMEM((most, 4, 2) + blocks, F32),
        pltpu.VMEM((most, 2, 2) + blocks, BF),
        pltpu.VMEM((most, 2, 2) + blocks, BF),
        pltpu.VMEM((most, 2, 4) + blocks, BF),
        dma((most, 8)), dma((most,)), dma((most,)),
        dma((most, 2)), dma((most, 2)),
        dma((most, 2, 2)), dma((most, 2, 2)),
        dma((most, 2, 4, QT)), dma((4,)),
    ]
    smem = pl.BlockSpec(memory_space=pltpu.SMEM)
    anywhere = pl.BlockSpec(memory_space=pl.ANY)
    return pl.pallas_call(
        functools.partial(kernel, n, chip_heads),
        out_shape=[jax.ShapeDtypeStruct((rows, width), BF)] * 4,
        in_specs=[smem, smem] + [anywhere] * 4,
        out_specs=[anywhere] * 4,
        scratch_shapes=scratch,
        compiler_params=pltpu.CompilerParams(
            collective_id=0, has_side_effects=True, vmem_limit_bytes=56 * 1024 * 1024
        ),
    )(tile_pattern, window, query, keys, values, grad_out)


def solution(mesh):
    rows = P(("tm", "head"), None)
    return jax.shard_map(
        functools.partial(shards, mesh.shape["tm"]),
        mesh=mesh,
        in_specs=(rows, rows, rows, rows, P(), P()),
        out_specs=(rows, rows, rows, rows),
        check_vma=False,
    )
```

```python
import functools
import math

import jax
import jax.numpy as jnp
from jax import lax
from jax.experimental import pallas as pl
from jax.experimental.pallas import tpu as pltpu
from jax.sharding import PartitionSpec as P

HD = 128
TILE = 128
QT = 4
SEL = 3
W = 3
QH = 2
QB = QT // QH * TILE
NEG = -1e30
SCALE = 1.0 / math.sqrt(HD)
FACTOR = SCALE / math.log(2.0)
MESH = pl.DeviceIdType.MESH
BF = jnp.bfloat16
F32 = jnp.float32


def kernel(
    n, chip_heads,
    pat_ref, win_ref, q_ref, k_ref, v_ref, g_ref,
    o_ref, dq_ref, dk_ref, dv_ref,
    qg, kv, bias, kt, vt, score, pt, dst, gs, acc, g_out, g_in, outb,
    in_send, kv_in, qg_in, next_send, next_in, g_send, g_recv, out_send, out_recv,
):
    f = lax.axis_index("tm")
    seat = lax.axis_index("head")
    half = n // 2
    pair, side = f // 2, lax.rem(f, 2)
    pairs = n // 2
    most = (chip_heads + 1) // 2

    def count(at):
        return (chip_heads + 1 - lax.rem(at, 2)) // 2

    def first_head(other, at):
        row = lax.rem(other + pair, 2)
        column = lax.rem(at // 2 + f // half, 2)
        return (row * 2 + column) * chip_heads + lax.rem(at, 2) * most

    def linked(step):
        frame = 2 * (pair + step) + 1 - side
        turn = (frame + n) // half - (f + n) // half
        return (frame, lax.rem(seat + 2 * turn + 2 * QT, QT))

    nxt, prv = linked(1), linked(-1)
    has_next = pair < pairs - 1
    has_prev = pair > 0
    mine = count(seat)
    peers = [(dx, dj) for dj in range(QT) for dx in (1, 0)]
    arrivals = [(dx, QT - dj if dj else 0) for dx, dj in peers]

    def peer(dx, dj):
        return lax.rem(side + dx, 2), lax.rem(seat + dj, QT)

    barrier = pltpu.get_barrier_semaphore()
    for dx, dj in peers:
        if dx or dj:
            other, at = peer(dx, dj)
            pl.semaphore_signal(barrier, inc=1, device_id=(2 * pair + other, at), device_id_type=MESH)

    @pl.when(has_next)
    def _():
        pl.semaphore_signal(barrier, inc=1, device_id=nxt, device_id_type=MESH)

    @pl.when(has_prev)
    def _():
        pl.semaphore_signal(barrier, inc=1, device_id=prv, device_id_type=MESH)

    pl.semaphore_wait(barrier, 2 * QT - 1 + (pair + pairs - 1) // pairs + (2 * pairs - 2 - pair) // pairs)

    def columns(head):
        return pl.ds(pl.multiple_of(head * HD, HD), HD)

    def wait_for(ref, sem):
        pltpu.make_async_copy(ref, ref, sem).wait()

    def send(src, dst, ssem, rsem, device):
        pltpu.make_async_remote_copy(
            src_ref=src, dst_ref=dst, send_sem=ssem, recv_sem=rsem,
            device_id=device, device_id_type=MESH,
        ).start()

    def enter(i, refs, slot, sem_of):
        for dx, dj in peers:
            other, at = peer(dx, dj)
            cols = columns(first_head(other, at) + i)

            @pl.when(i < count(at))
            def _():
                sem = sem_of(dx, dj)
                for a, ref in enumerate(refs):
                    if dx or dj:
                        send(ref.at[:, cols], slot.at[a, seat], in_send.at[i, 2 * dj + dx], sem,
                             (2 * pair + other, at))
                    else:
                        pltpu.make_async_copy(ref.at[:, cols], slot.at[a, seat], sem).start()

    def enter_kv(i):
        enter(i, (k_ref, v_ref), kv.at[i, 1 - side],
              lambda dx, dj: kv_in.at[i, 2 * ((QT - dj) % QT) + dx])

    enter_kv(0)

    @pl.when(has_next)
    def _():
        @pl.loop(0, mine)
        def _(i):
            for a, ref in enumerate((k_ref, v_ref)):
                send(ref.at[:, columns(first_head(side, seat) + i)], kv.at[i, 3 - side, a, seat],
                     next_send.at[i, 1 - side], next_in.at[i, 1 - side], nxt)

    def enter_qg(i):
        enter(i, (q_ref, g_ref), qg.at[i, side], lambda dx, dj: qg_in.at[i])

    if most > 1:
        enter_kv(1)

    lane = lax.broadcasted_iota(jnp.int32, (1, QB), 1)
    for x in range(2):
        frame = 2 * pair + x
        limit = win_ref[frame]
        for h in range(QH):
            for lag in range(W):
                for t in range(QT):
                    both = []
                    for tile in (2 * h, 2 * h + 1):
                        hit = pat_ref[lag, tile, 0] == t
                        for s in range(1, SEL):
                            hit = hit | (pat_ref[lag, tile, s] == t)
                        hit = hit & (lag <= frame) & (lag < limit)
                        both.append(jnp.where(hit, 0.0, NEG).astype(F32))
                    bias[x, h, lag * QT + t] = jnp.where(lane < TILE, both[0], both[1])

    @pl.loop(0, most)
    def _(i):
        acc[i] = jnp.zeros(acc.shape[1:], F32)

        @pl.when(pair == 0)
        def _():
            kv[i, 2] = jnp.zeros(kv.shape[2:], BF)
            kv[i, 3] = jnp.zeros(kv.shape[2:], BF)

        @pl.when(pair == pairs - 1)
        def _():
            g_in[i] = jnp.zeros(g_in.shape[1:], BF)

    def own(i):
        for dx, dj in arrivals:
            other, tile = peer(dx, dj)
            s = 1 - other
            for_tile = kv.at[i, s, :, tile]
            wait_for(for_tile, kv_in.at[i, 2 * dj + dx])
            if dx or dj:
                @pl.when(has_next)
                def _():
                    send(for_tile, kv.at[i, 2 + s, :, tile], next_send.at[i, s], next_in.at[i, s], nxt)

    def leave(i, x, a):
        ref = (o_ref, dq_ref, dk_ref, dv_ref)[a]
        where_to = ref.at[:, columns(first_head(side, seat) + i)]
        for dj in range(QT):
            at = lax.rem(seat + dj, QT)
            if dj:
                send(outb.at[i, x, a, at], where_to, out_send.at[i, x, a, dj], out_recv.at[a],
                     (2 * pair + x, at))
            else:
                @pl.when(x == side)
                def _():
                    pltpu.make_async_copy(outb.at[i, x, a, at], where_to, out_recv.at[a]).start()

                @pl.when(x != side)
                def _():
                    send(outb.at[i, x, a, at], where_to, out_send.at[i, x, a, dj], out_recv.at[a],
                         (2 * pair + 1 - side, at))

    def nt(a, b):
        return lax.dot_general(a, b, (((1,), (1,)), ((), ())), preferred_element_type=F32)

    def mm(a, b):
        return jnp.dot(a, b, preferred_element_type=F32)

    def fold(block, op):
        return op(block.reshape(TILE // 8, 8, QB), axis=0)

    def attend(i, x):
        base = 1 - x

        def turn(slot):
            kt[slot] = kv[i, slot, 0].reshape(QT * TILE, HD).T
            vt[slot] = kv[i, slot, 1].reshape(QT * TILE, HD).T

        @pl.when(x == 1)
        def _():
            for slot in range(3):
                turn(slot)

        @pl.when(x == 0)
        def _():
            turn(3)

        for h in range(QH):
            lanes = slice(h * QB, (h + 1) * QB)
            qh = qg[i, x, 0, 2 * h:2 * h + 2].reshape(QB, HD)
            gh = qg[i, x, 1, 2 * h:2 * h + 2].reshape(QB, HD)
            top = None
            for lag in range(W):
                for t in range(QT):
                    r = lag * QT + t
                    s = nt(kv[i, base + lag, 0, t], qh)
                    score[h, r] = s
                    here = fold(s, jnp.max) + bias[x, h, r]
                    top = here if top is None else jnp.maximum(top, here)
            top = jnp.max(top, axis=0, keepdims=True)
            total = None
            for r in range(W * QT):
                e = jnp.exp2(score[h, r] * FACTOR + (bias[x, h, r] - top) * FACTOR)
                pt[r, :, lanes] = e.astype(BF)
                here = fold(e, jnp.sum)
                total = here if total is None else total + here
            inverse = 1.0 / jnp.sum(total, axis=0, keepdims=True)
            out = None
            for lag in range(W):
                probs = pt[lag * QT:(lag + 1) * QT, :, lanes].reshape(QT * TILE, QB)
                here = mm(vt[base + lag], probs)
                out = here if out is None else out + here
            out = out * inverse
            scaled = (gh.T.astype(F32) * inverse).astype(BF)
            delta = jnp.sum(scaled.astype(F32) * out, axis=0, keepdims=True)
            outb[i, x, 0, 2 * h:2 * h + 2] = out.astype(BF).T.reshape(2, TILE, HD)
            back = scaled.T
            gs[lanes] = back
            for lag in range(W):
                for t in range(QT):
                    r = lag * QT + t
                    dp = nt(kv[i, base + lag, 1, t], back) - delta
                    dst[r, :, lanes] = dp.astype(BF) * pt[r, :, lanes]
            dq = None
            for lag in range(W):
                ds = dst[lag * QT:(lag + 1) * QT, :, lanes].reshape(QT * TILE, QB)
                here = mm(kt[base + lag], ds)
                dq = here if dq is None else dq + here
            outb[i, x, 1, 2 * h:2 * h + 2] = (dq * SCALE).astype(BF).T.reshape(2, TILE, HD)

        rows = qg[i, x, 0].reshape(QT * TILE, HD)
        for lag in range(W):
            block = dst[lag * QT:(lag + 1) * QT].reshape(QT * TILE, QT * TILE)
            acc[i, base + lag, 0] += (mm(block, rows) * SCALE).reshape(QT, TILE, HD)
            block = pt[lag * QT:(lag + 1) * QT].reshape(QT * TILE, QT * TILE)
            acc[i, base + lag, 1] += mm(block, gs[...]).reshape(QT, TILE, HD)

    def finish(i):
        for s in range(2):
            for a in range(2):
                @pl.when(has_next)
                def _():
                    wait_for(g_in.at[i, s, a], g_recv.at[i, s, a])

                outb[i, 1 - s, 2 + a] = (acc[i, s, a] + g_in[i, s, a].astype(F32)).astype(BF)
                leave(i, 1 - s, 2 + a)

    own(0)
    enter_qg(0)

    @pl.when(1 < mine)
    def _():
        own(1)

    @pl.loop(1, most)
    def _(i):
        @pl.when(i + 1 < most)
        def _():
            enter_kv(i + 1)

        enter_qg(i)

    @pl.loop(0, 2 * most + 2)
    def _(u):
        i, odd = u // 2, lax.rem(u, 2)

        @pl.when(i < mine)
        def _():
            @pl.when(odd == 0)
            def _():
                wait_for(qg.at[i], qg_in.at[i])

            @pl.when(has_prev)
            def _():
                wait_for(kv.at[i, 2 + odd], next_in.at[i, odd])

            attend(i, 1 - odd)
            leave(i, 1 - odd, 0)
            leave(i, 1 - odd, 1)

            @pl.when((odd == 1) & has_prev)
            def _():
                for s in range(2):
                    for a in range(2):
                        g_out[i, s, a] = acc[i, 2 + s, a].astype(BF)
                        send(g_out.at[i, s, a], g_in.at[i, s, a], g_send.at[i, s, a],
                             g_recv.at[i, s, a], prv)

        @pl.when((odd == 0) & (i + 2 < mine))
        def _():
            own(i + 2)

        @pl.when((odd == 1) & (i >= 1) & (i < mine + 1))
        def _():
            finish(i - 1)

    @pl.loop(0, most)
    def _(i):
        for dx, dj in peers:
            if dx or dj:
                @pl.when(i < count(peer(dx, dj)[1]))
                def _():
                    wait_for(qg.at[i, 0, 0], in_send.at[i, 2 * dj + dx])

        @pl.when(i < mine)
        def _():
            for x in range(2):
                for a in range(4):
                    for dj in range(QT):
                        if dj:
                            wait_for(outb.at[i, x, a, dj], out_send.at[i, x, a, dj])
                        else:
                            @pl.when(x != side)
                            def _():
                                wait_for(outb.at[i, x, a, dj], out_send.at[i, x, a, dj])

            for s in range(2):
                @pl.when(has_next)
                def _():
                    wait_for(kv.at[i, s], next_send.at[i, s])

                @pl.when(has_prev)
                def _():
                    for a in range(2):
                        wait_for(g_out.at[i, s, a], g_send.at[i, s, a])

    for a, ref in enumerate((o_ref, dq_ref, dk_ref, dv_ref)):
        wait_for(ref, out_recv.at[a])


def shards(n, query, keys, values, grad_out, tile_pattern, window):
    rows, width = query.shape
    chip_heads = width // HD // 4
    most = (chip_heads + 1) // 2
    blocks = (QT, TILE, HD)
    dma = pltpu.SemaphoreType.DMA
    scratch = [
        pltpu.VMEM((most, 2, 2) + blocks, BF),
        pltpu.VMEM((most, 4, 2) + blocks, BF),
        pltpu.VMEM((2, QH, W * QT, 1, QB), F32),
        pltpu.VMEM((4, HD, QT * TILE), BF),
        pltpu.VMEM((4, HD, QT * TILE), BF),
        pltpu.VMEM((QH, W * QT, TILE, QB), F32),
        pltpu.VMEM((W * QT, TILE, QT * TILE), BF),
        pltpu.VMEM((W * QT, TILE, QT * TILE), BF),
        pltpu.VMEM((QT * TILE, HD), BF),
        pltpu.VMEM((most, 4, 2) + blocks, F32),
        pltpu.VMEM((most, 2, 2) + blocks, BF),
        pltpu.VMEM((most, 2, 2) + blocks, BF),
        pltpu.VMEM((most, 2, 4) + blocks, BF),
        dma((most, 8)), dma((most, 8)), dma((most,)),
        dma((most, 2)), dma((most, 2)),
        dma((most, 2, 2)), dma((most, 2, 2)),
        dma((most, 2, 4, QT)), dma((4,)),
    ]
    smem = pl.BlockSpec(memory_space=pltpu.SMEM)
    anywhere = pl.BlockSpec(memory_space=pl.ANY)
    return pl.pallas_call(
        functools.partial(kernel, n, chip_heads),
        out_shape=[pltpu.VMEM((rows, width), BF)] * 4,
        in_specs=[smem, smem] + [anywhere] * 4,
        out_specs=[pl.BlockSpec(memory_space=pltpu.VMEM)] * 4,
        scratch_shapes=scratch,
        compiler_params=pltpu.CompilerParams(
            collective_id=0, has_side_effects=True, vmem_limit_bytes=56 * 1024 * 1024
        ),
    )(tile_pattern, window, query, keys, values, grad_out)


def solution(mesh):
    rows = P(("tm", "head"), None)
    return jax.shard_map(
        functools.partial(shards, mesh.shape["tm"]),
        mesh=mesh,
        in_specs=(rows, rows, rows, rows, P(), P()),
        out_specs=(rows, rows, rows, rows),
        check_vma=False,
    )
```

```python
import functools
import math

import jax
import jax.numpy as jnp
from jax import lax
from jax.experimental import pallas as pl
from jax.experimental.pallas import tpu as pltpu
from jax.sharding import PartitionSpec as P

HD = 128
TILE = 128
QT = 4
SEL = 3
W = 3
QH = 2
QB = QT // QH * TILE
NEG = -1e30
SCALE = 1.0 / math.sqrt(HD)
FACTOR = SCALE / math.log(2.0)
MESH = pl.DeviceIdType.MESH
BF = jnp.bfloat16
F32 = jnp.float32


def kernel(
    n,
    pat_ref, win_ref, q_ref, k_ref, v_ref, g_ref,
    o_ref, dq_ref, dk_ref, dv_ref,
    qg, kv, bias, kt, vt, score, pt, dst, gs, acc, g_out, g_in, outb,
    full_send, half_send, kv_in, qg_in, next_send, next_in, g_send, g_recv, out_send, out_recv,
):
    f = lax.axis_index("tm")
    seat = lax.axis_index("head")
    half = n // 2
    rows = n // 4
    row, x = f // 4, lax.rem(f, 4)
    pair, core = x // 2, lax.rem(seat, 2)
    upper = f // half
    full_heads = 4 * QT

    def column_of(at):
        return lax.rem(at // 2 + upper, 2)

    def full_head(other, at):
        return other * 4 + column_of(at) * 2 + lax.rem(at, 2)

    def half_at(e, p):
        return e % 2 + p * (3 - 2 * (e % 2)), 2 * lax.rem(e // 2 + upper, 2)

    my_head = (full_head(x, seat), full_heads + lax.rem(x + pair, 2) + 2 * column_of(seat))

    def device(frame):
        turn = (frame + n) // half - (f + n) // half
        return (frame, lax.rem(seat + 2 * turn + 2 * QT, QT))

    nxt = (device(f + 4), device(4 * (row + pair) + 3 - x))
    prv = (device(f - 4), device(4 * (row + pair - 1) + 3 - x))
    has_next = (row < rows - 1, 2 * row + pair < 2 * rows - 1)
    has_prev = (row > 0, 2 * row + pair > 0)

    def each_job(job, action):
        for at in range(2):
            @pl.when(job == at)
            def _():
                action(at)

    barrier = pltpu.get_barrier_semaphore()

    def greet(who):
        pl.semaphore_signal(barrier, inc=1, device_id=who, device_id_type=MESH)

    for dx in range(4):
        for dj in range(QT):
            if dx or dj:
                greet((4 * row + lax.rem(x + dx, 4), lax.rem(seat + dj, QT)))

    @pl.when(has_next[0])
    def _():
        greet(nxt[0])

    @pl.when(has_prev[0])
    def _():
        greet(prv[0])

    @pl.when((pair == 1) & has_next[0])
    def _():
        greet(nxt[1])

    @pl.when((pair == 0) & has_prev[0])
    def _():
        greet(prv[1])

    not_first = (row + rows - 1) // rows
    not_last = (2 * rows - 2 - row) // rows
    pl.semaphore_wait(barrier, 15 + (2 - pair) * not_first + (1 + pair) * not_last)

    def columns(head):
        return pl.ds(pl.multiple_of(head * HD, HD), HD)

    def wait_for(ref, sem):
        pltpu.make_async_copy(ref, ref, sem).wait()

    def send(src, dst, ssem, rsem, device):
        pltpu.make_async_remote_copy(
            src_ref=src, dst_ref=dst, send_sem=ssem, recv_sem=rsem,
            device_id=device, device_id_type=MESH,
        ).start()

    def place(refs, head, slot, ssem, rsem, other, at, local):
        cols = columns(head)
        if local is not False:
            @pl.when(local)
            def _():
                for a, ref in enumerate(refs):
                    pltpu.make_async_copy(ref.at[:, cols], slot.at[a, seat], rsem).start()

        @pl.when(True if local is False else jnp.logical_not(local))
        def _():
            for a, ref in enumerate(refs):
                send(ref.at[:, cols], slot.at[a, seat], ssem, rsem, (4 * row + other, at))

    side = lax.rem(x, 2)

    def enter_full(refs, slot, rsem, parity):
        for dx in (2, 1, 3, 0):
            for at in (parity, parity + 2):
                other = lax.rem(x + dx, 4)
                place(refs, full_head(other, at), slot, full_send.at[dx, at], rsem,
                      other, at, False if dx else seat == at)

    def enter_half(refs, slot, rsem):
        for e in range(4):
            other, at = half_at(e, pair)
            place(refs, full_heads + e, slot, half_send.at[e], rsem,
                  other, at, (other == x) & (at == seat))

    keys, tops = (k_ref, v_ref), (q_ref, g_ref)

    def full_kv(parity):
        enter_full(keys, kv.at[0, 3 - x], kv_in.at[0, 3 - x], parity)

    def full_qg(parity):
        enter_full(tops, qg.at[0, x], qg_in.at[0, x], parity)

    def own(job):
        for s in range(4 - 2 * job):
            wait_for(kv.at[job, s], kv_in.at[job, s])
            if s < 2:
                @pl.when(has_next[job])
                def _():
                    send(kv.at[job, s], kv.at[job, 4 - 2 * job + s],
                         next_send.at[job, s], next_in.at[job, s], nxt[job])

    full_kv(0)
    full_qg(0)
    enter_half(keys, kv.at[1, 1 - side], kv_in.at[1, 1 - side])

    lane = lax.broadcasted_iota(jnp.int32, (1, QB), 1)

    @pl.loop(0, 4)
    def _(fx):
        frame = 4 * row + fx
        limit = win_ref[frame]
        for h in range(QH):
            for lag in range(W):
                for t in range(QT):
                    both = []
                    for tile in (2 * h, 2 * h + 1):
                        hit = pat_ref[lag, tile, 0] == t
                        for s in range(1, SEL):
                            hit = hit | (pat_ref[lag, tile, s] == t)
                        hit = hit & (lag <= frame) & (lag < limit)
                        both.append(jnp.where(hit, 0.0, NEG).astype(F32))
                    bias[fx, h, lag * QT + t] = jnp.where(lane < TILE, both[0], both[1])

    full_kv(1)

    @pl.loop(0, 2)
    def _(job):
        @pl.loop(0, 6)
        def _(s):
            acc[job, s] = jnp.zeros(acc.shape[2:], F32)

    for job in range(2):
        for s in range(2):
            @pl.when(jnp.logical_not(has_prev[job]))
            def _():
                kv[job, 4 - 2 * job + s] = jnp.zeros(kv.shape[2:], BF)

            @pl.when(jnp.logical_not(has_next[job]))
            def _():
                g_in[job, s] = jnp.zeros(g_in.shape[2:], BF)

    @pl.when(core == 0)
    def _():
        own(0)

    full_qg(1)
    enter_half(tops, qg.at[1, side], qg_in.at[1, side])

    @pl.when(core == 1)
    def _():
        own(0)

    def leave(job, fr, a):
        ref = (o_ref, dq_ref, dk_ref, dv_ref)[a]
        where_to = ref.at[:, columns(jnp.where(job == 0, my_head[0], my_head[1]))]
        owner = fr + 2 * pair * job
        for dj in range(QT):
            at = lax.rem(seat + dj, QT)
            src = outb.at[job, fr, a, at]
            if dj:
                send(src, where_to, out_send.at[job, fr, a, dj], out_recv.at[a], (4 * row + owner, at))
            else:
                @pl.when(owner == x)
                def _():
                    pltpu.make_async_copy(src, where_to, out_recv.at[a]).start()

                @pl.when(owner != x)
                def _():
                    send(src, where_to, out_send.at[job, fr, a, dj], out_recv.at[a], (4 * row + owner, at))

    def nt(a, b):
        return lax.dot_general(a, b, (((1,), (1,)), ((), ())), preferred_element_type=F32)

    def mm(a, b):
        return jnp.dot(a, b, preferred_element_type=F32)

    def fold(block, op):
        return op(block.reshape(TILE // 8, 8, QB), axis=0)

    def attend(i, fr, base, x):

        def turn(slot):
            kt[slot] = kv[i, slot, 0].reshape(QT * TILE, HD).T
            vt[slot] = kv[i, slot, 1].reshape(QT * TILE, HD).T

        @pl.when(base == 0)
        def _():
            turn(0)
            turn(1)

        turn(base + 2)

        for h in range(QH):
            lanes = slice(h * QB, (h + 1) * QB)
            qh = qg[i, fr, 0, 2 * h:2 * h + 2].reshape(QB, HD)
            gh = qg[i, fr, 1, 2 * h:2 * h + 2].reshape(QB, HD)
            top = None
            for lag in range(W):
                for t in range(QT):
                    r = lag * QT + t
                    s = nt(kv[i, base + lag, 0, t], qh)
                    score[h, r] = s
                    here = fold(s, jnp.max) + bias[x, h, r]
                    top = here if top is None else jnp.maximum(top, here)
            top = jnp.max(top, axis=0, keepdims=True)
            total = None
            for r in range(W * QT):
                e = jnp.exp2(score[h, r] * FACTOR + (bias[x, h, r] - top) * FACTOR)
                pt[r, :, lanes] = e.astype(BF)
                here = fold(e, jnp.sum)
                total = here if total is None else total + here
            inverse = 1.0 / jnp.sum(total, axis=0, keepdims=True)
            out = None
            for lag in range(W):
                probs = pt[lag * QT:(lag + 1) * QT, :, lanes].reshape(QT * TILE, QB)
                here = mm(vt[base + lag], probs)
                out = here if out is None else out + here
            out = out * inverse
            scaled = (gh.T.astype(F32) * inverse).astype(BF)
            delta = jnp.sum(scaled.astype(F32) * out, axis=0, keepdims=True)
            outb[i, fr, 0, 2 * h:2 * h + 2] = out.astype(BF).T.reshape(2, TILE, HD)
            back = scaled.T
            gs[lanes] = back
            for lag in range(W):
                for t in range(QT):
                    r = lag * QT + t
                    dp = nt(kv[i, base + lag, 1, t], back) - delta
                    dst[r, :, lanes] = dp.astype(BF) * pt[r, :, lanes]
            dq = None
            for lag in range(W):
                ds = dst[lag * QT:(lag + 1) * QT, :, lanes].reshape(QT * TILE, QB)
                here = mm(kt[base + lag], ds)
                dq = here if dq is None else dq + here
            outb[i, fr, 1, 2 * h:2 * h + 2] = (dq * SCALE).astype(BF).T.reshape(2, TILE, HD)

        rows = qg[i, fr, 0].reshape(QT * TILE, HD)
        for lag in range(W):
            block = dst[lag * QT:(lag + 1) * QT].reshape(QT * TILE, QT * TILE)
            acc[i, base + lag, 0] += (mm(block, rows) * SCALE).reshape(QT, TILE, HD)
            block = pt[lag * QT:(lag + 1) * QT].reshape(QT * TILE, QT * TILE)
            acc[i, base + lag, 1] += mm(block, gs[...]).reshape(QT, TILE, HD)

    def back(job):
        @pl.when(has_prev[job])
        def _():
            for s in range(2):
                for a in range(2):
                    g_out[job, s, a] = acc[job, 4 - 2 * job + s, a].astype(BF)
                    send(g_out.at[job, s, a], g_in.at[job, s, a], g_send.at[job, s, a],
                         g_recv.at[job, s, a], prv[job])

    def finish(job):
        for s in range(2):
            for a in range(2):
                @pl.when(has_next[job])
                def _():
                    wait_for(g_in.at[job, s, a], g_recv.at[job, s, a])

                fr = 3 - 2 * job - s
                outb[job, fr, 2 + a] = (acc[job, s, a] + g_in[job, s, a].astype(F32)).astype(BF)
                leave(job, fr, 2 + a)

    units = 6 - 2 * core

    @pl.loop(0, units)
    def _(u):
        job = u // 4
        base = u - 4 * job
        fr = 3 - u + 2 * job
        wait_for(qg.at[job, fr], qg_in.at[job, fr])

        def arrived(at):
            @pl.when(has_prev[at])
            def _():
                s = lax.rem(u, 2)
                wait_for(kv.at[at, 4 - 2 * at + s], next_in.at[at, s])

        @pl.when(u >= 2)
        def _():
            each_job(job, arrived)

        attend(job, fr, base, fr + 2 * pair * job)
        leave(job, fr, 0)
        leave(job, fr, 1)

        @pl.when((u == 1) & (core == 0))
        def _():
            own(1)

        @pl.when((u == 2) | (u == 3))
        def _():
            for a in range(2):
                outb[0, fr, 2 + a] = acc[0, u, a].astype(BF)
                leave(0, fr, 2 + a)

        @pl.when((u == 3) | (u == 5))
        def _():
            each_job(job, back)

    finish(0)

    @pl.when(core == 0)
    def _():
        finish(1)

    for at in range(QT):
        for dx in range(4):
            if dx:
                wait_for(qg.at[0, 0, 0], full_send.at[dx, at])
            else:
                @pl.when(at != seat)
                def _():
                    wait_for(qg.at[0, 0, 0], full_send.at[dx, at])

    for e in range(4):
        other, at = half_at(e, pair)

        @pl.when(jnp.logical_not((other == x) & (at == seat)))
        def _():
            wait_for(qg.at[0, 0, 0], half_send.at[e])

    @pl.loop(0, 2 - core)
    def _(job):
        @pl.loop(0, 4 - 2 * job)
        def _(fr):
            for a in range(4):
                for dj in range(QT):
                    if dj:
                        wait_for(outb.at[job, fr, a, dj], out_send.at[job, fr, a, dj])
                    else:
                        @pl.when(fr + 2 * pair * job != x)
                        def _():
                            wait_for(outb.at[job, fr, a, dj], out_send.at[job, fr, a, dj])

    def sent(job):
        for s in range(2):
            @pl.when(has_next[job])
            def _():
                wait_for(kv.at[job, s], next_send.at[job, s])

            @pl.when(has_prev[job])
            def _():
                for a in range(2):
                    wait_for(g_out.at[job, s, a], g_send.at[job, s, a])

    sent(0)

    @pl.when(core == 0)
    def _():
        sent(1)

    for a, ref in enumerate((o_ref, dq_ref, dk_ref, dv_ref)):
        wait_for(ref, out_recv.at[a])


def shards(n, query, keys, values, grad_out, tile_pattern, window):
    rows, width = query.shape
    blocks = (QT, TILE, HD)
    dma = pltpu.SemaphoreType.DMA
    scratch = [
        pltpu.VMEM((2, 4, 2) + blocks, BF),
        pltpu.VMEM((2, 6, 2) + blocks, BF),
        pltpu.VMEM((4, QH, W * QT, 1, QB), F32),
        pltpu.VMEM((6, HD, QT * TILE), BF),
        pltpu.VMEM((6, HD, QT * TILE), BF),
        pltpu.VMEM((QH, W * QT, TILE, QB), F32),
        pltpu.VMEM((W * QT, TILE, QT * TILE), BF),
        pltpu.VMEM((W * QT, TILE, QT * TILE), BF),
        pltpu.VMEM((QT * TILE, HD), BF),
        pltpu.VMEM((2, 6, 2) + blocks, F32),
        pltpu.VMEM((2, 2, 2) + blocks, BF),
        pltpu.VMEM((2, 2, 2) + blocks, BF),
        pltpu.VMEM((2, 4, 4) + blocks, BF),
        dma((4, QT)), dma((4,)), dma((2, 4)), dma((2, 4)),
        dma((2, 2)), dma((2, 2)),
        dma((2, 2, 2)), dma((2, 2, 2)),
        dma((2, 4, 4, QT)), dma((4,)),
    ]
    smem = pl.BlockSpec(memory_space=pltpu.SMEM)
    anywhere = pl.BlockSpec(memory_space=pl.ANY)
    return pl.pallas_call(
        functools.partial(kernel, n),
        out_shape=[pltpu.VMEM((rows, width), BF)] * 4,
        in_specs=[smem, smem] + [anywhere] * 4,
        out_specs=[pl.BlockSpec(memory_space=pltpu.VMEM)] * 4,
        scratch_shapes=scratch,
        compiler_params=pltpu.CompilerParams(
            collective_id=0, has_side_effects=True, vmem_limit_bytes=56 * 1024 * 1024
        ),
    )(tile_pattern, window, query, keys, values, grad_out)


def solution(mesh):
    rows = P(("tm", "head"), None)
    return jax.shard_map(
        functools.partial(shards, mesh.shape["tm"]),
        mesh=mesh,
        in_specs=(rows, rows, rows, rows, P(), P()),
        out_specs=(rows, rows, rows, rows),
        check_vma=False,
    )
```

```python
import functools
import math

import jax
import jax.numpy as jnp
from jax import lax
from jax.experimental import pallas as pl
from jax.experimental.pallas import tpu as pltpu
from jax.sharding import PartitionSpec as P

HD = 128
TILE = 128
QT = 4
SEL = 3
W = 3
QH = 2
QB = QT // QH * TILE
NEG = -1e30
SCALE = 1.0 / math.sqrt(HD)
FACTOR = SCALE / math.log(2.0)
MESH = pl.DeviceIdType.MESH
BF = jnp.bfloat16
F32 = jnp.float32


def kernel(
    n,
    pat_ref, win_ref, q_ref, k_ref, v_ref, g_ref,
    o_ref, dq_ref, dk_ref, dv_ref,
    qg, kv, bias, kt, vt, score, pt, dst, gs, acc, g_out, g_in, outb,
    full_send, half_send, kv_in, qg_in, next_send, next_in, g_send, g_recv, out_send, out_recv,
):
    f = lax.axis_index("tm")
    seat = lax.axis_index("head")
    half = n // 2
    rows = n // 4
    row, x = f // 4, lax.rem(f, 4)
    pair, core = x // 2, lax.rem(seat, 2)
    upper = f // half
    full_heads = 4 * QT

    def column_of(at):
        return lax.rem(at // 2 + upper, 2)

    def full_head(other, at):
        return other * 4 + column_of(at) * 2 + lax.rem(at, 2)

    def half_at(e, p):
        return e % 2 + p * (3 - 2 * (e % 2)), 2 * lax.rem(e // 2 + upper, 2)

    my_head = (full_head(x, seat), full_heads + lax.rem(x + pair, 2) + 2 * column_of(seat))

    def device(frame):
        turn = (frame + n) // half - (f + n) // half
        return (frame, lax.rem(seat + 2 * turn + 2 * QT, QT))

    nxt = (device(f + 4), device(4 * (row + pair) + 3 - x))
    prv = (device(f - 4), device(4 * (row + pair - 1) + 3 - x))
    has_next = (row < rows - 1, 2 * row + pair < 2 * rows - 1)
    has_prev = (row > 0, 2 * row + pair > 0)

    def each_job(job, action):
        for at in range(2):
            @pl.when(job == at)
            def _():
                action(at)

    barrier = pltpu.get_barrier_semaphore()

    def greet(who):
        pl.semaphore_signal(barrier, inc=1, device_id=who, device_id_type=MESH)

    for dx in range(4):
        for dj in range(QT):
            if dx or dj:
                greet((4 * row + lax.rem(x + dx, 4), lax.rem(seat + dj, QT)))

    @pl.when(has_next[0])
    def _():
        greet(nxt[0])

    @pl.when(has_prev[0])
    def _():
        greet(prv[0])

    @pl.when((pair == 1) & has_next[0])
    def _():
        greet(nxt[1])

    @pl.when((pair == 0) & has_prev[0])
    def _():
        greet(prv[1])

    not_first = (row + rows - 1) // rows
    not_last = (2 * rows - 2 - row) // rows
    pl.semaphore_wait(barrier, 15 + (2 - pair) * not_first + (1 + pair) * not_last)

    def columns(head):
        return pl.ds(pl.multiple_of(head * HD, HD), HD)

    def wait_for(ref, sem):
        pltpu.make_async_copy(ref, ref, sem).wait()

    def send(src, dst, ssem, rsem, device):
        pltpu.make_async_remote_copy(
            src_ref=src, dst_ref=dst, send_sem=ssem, recv_sem=rsem,
            device_id=device, device_id_type=MESH,
        ).start()

    def place(refs, head, slot, ssem, rsem, other, at, local):
        cols = columns(head)
        if local is not False:
            @pl.when(local)
            def _():
                for a, ref in enumerate(refs):
                    pltpu.make_async_copy(ref.at[:, cols], slot.at[a, seat], rsem).start()

        @pl.when(True if local is False else jnp.logical_not(local))
        def _():
            for a, ref in enumerate(refs):
                send(ref.at[:, cols], slot.at[a, seat], ssem, rsem, (4 * row + other, at))

    side = lax.rem(x, 2)

    def enter_full(refs, slot, rsem, parity):
        for dx in (2, 1, 3, 0):
            for at in (parity, parity + 2):
                other = lax.rem(x + dx, 4)
                place(refs, full_head(other, at), slot, full_send.at[dx, at], rsem,
                      other, at, False if dx else seat == at)

    def enter_half(refs, slot, rsem):
        for e in range(4):
            other, at = half_at(e, pair)
            place(refs, full_heads + e, slot, half_send.at[e], rsem,
                  other, at, (other == x) & (at == seat))

    keys, tops = (k_ref, v_ref), (q_ref, g_ref)

    def full_kv(parity):
        enter_full(keys, kv.at[0, 3 - x], kv_in.at[0, 3 - x], parity)

    def full_qg(parity):
        enter_full(tops, qg.at[0, x], qg_in.at[0, x], parity)

    def own(job):
        for s in range(4 - 2 * job):
            wait_for(kv.at[job, s], kv_in.at[job, s])
            if s < 2:
                @pl.when(has_next[job])
                def _():
                    send(kv.at[job, s], kv.at[job, 4 - 2 * job + s],
                         next_send.at[job, s], next_in.at[job, s], nxt[job])

    full_kv(0)
    full_qg(0)
    enter_half(keys, kv.at[1, 1 - side], kv_in.at[1, 1 - side])

    lane = lax.broadcasted_iota(jnp.int32, (1, QB), 1)

    @pl.loop(0, 4)
    def _(fx):
        frame = 4 * row + fx
        limit = win_ref[frame]
        for h in range(QH):
            for lag in range(W):
                for t in range(QT):
                    both = []
                    for tile in (2 * h, 2 * h + 1):
                        hit = pat_ref[lag, tile, 0] == t
                        for s in range(1, SEL):
                            hit = hit | (pat_ref[lag, tile, s] == t)
                        hit = hit & (lag <= frame) & (lag < limit)
                        both.append(jnp.where(hit, 0.0, NEG).astype(F32))
                    bias[fx, h, lag * QT + t] = jnp.where(lane < TILE, both[0], both[1])

    full_kv(1)

    @pl.loop(0, 2)
    def _(job):
        @pl.loop(0, 6)
        def _(s):
            acc[job, s] = jnp.zeros(acc.shape[2:], F32)

    for job in range(2):
        for s in range(2):
            @pl.when(jnp.logical_not(has_prev[job]))
            def _():
                kv[job, 4 - 2 * job + s] = jnp.zeros(kv.shape[2:], BF)

            @pl.when(jnp.logical_not(has_next[job]))
            def _():
                g_in[job, s] = jnp.zeros(g_in.shape[2:], BF)

    @pl.when(core == 0)
    def _():
        own(0)

    full_qg(1)
    enter_half(tops, qg.at[1, side], qg_in.at[1, side])

    @pl.when(core == 1)
    def _():
        own(0)

    def leave(job, fr, a):
        ref = (o_ref, dq_ref, dk_ref, dv_ref)[a]
        where_to = ref.at[:, columns(jnp.where(job == 0, my_head[0], my_head[1]))]
        owner = fr + 2 * pair * job
        for dj in range(QT):
            at = lax.rem(seat + dj, QT)
            src = outb.at[job, fr, a, at]
            if dj:
                send(src, where_to, out_send.at[job, fr, a, dj], out_recv.at[a], (4 * row + owner, at))
            else:
                @pl.when(owner == x)
                def _():
                    pltpu.make_async_copy(src, where_to, out_recv.at[a]).start()

                @pl.when(owner != x)
                def _():
                    send(src, where_to, out_send.at[job, fr, a, dj], out_recv.at[a], (4 * row + owner, at))

    def nt(a, b):
        return lax.dot_general(a, b, (((1,), (1,)), ((), ())), preferred_element_type=F32)

    def mm(a, b):
        return jnp.dot(a, b, preferred_element_type=F32)

    def fold(block, op):
        return op(block.reshape(TILE // 8, 8, QB), axis=0)

    def attend(i, fr, base, x, first):

        def turn(slot):
            kt[slot] = kv[i, slot, 0].reshape(QT * TILE, HD).T
            vt[slot] = kv[i, slot, 1].reshape(QT * TILE, HD).T

        turn(base)

        @pl.when(first)
        def _():
            turn(base + 1)
            turn(base + 2)

        for h in range(QH):
            lanes = slice(h * QB, (h + 1) * QB)
            qh = qg[i, fr, 0, 2 * h:2 * h + 2].reshape(QB, HD)
            gh = qg[i, fr, 1, 2 * h:2 * h + 2].reshape(QB, HD)
            top = None
            for lag in range(W):
                block = nt(kv[i, base + lag, 0].reshape(QT * TILE, HD), qh)
                for t in range(QT):
                    r = lag * QT + t
                    s = block[t * TILE:(t + 1) * TILE]
                    score[h, r] = s
                    here = fold(s, jnp.max) + bias[x, h, r]
                    top = here if top is None else jnp.maximum(top, here)
            top = jnp.max(top, axis=0, keepdims=True)
            total = None
            for r in range(W * QT):
                e = jnp.exp2(score[h, r] * FACTOR + (bias[x, h, r] - top) * FACTOR)
                pt[r, :, lanes] = e.astype(BF)
                here = fold(e, jnp.sum)
                total = here if total is None else total + here
            inverse = 1.0 / jnp.sum(total, axis=0, keepdims=True)
            out = None
            for lag in range(W):
                probs = pt[lag * QT:(lag + 1) * QT, :, lanes].reshape(QT * TILE, QB)
                here = mm(vt[base + lag], probs)
                out = here if out is None else out + here
            out = out * inverse
            scaled = (gh.T.astype(F32) * inverse).astype(BF)
            delta = jnp.sum(scaled.astype(F32) * out, axis=0, keepdims=True)
            outb[i, fr, 0, 2 * h:2 * h + 2] = out.astype(BF).T.reshape(2, TILE, HD)
            back = scaled.T
            gs[lanes] = back
            for lag in range(W):
                block = nt(kv[i, base + lag, 1].reshape(QT * TILE, HD), back)
                for t in range(QT):
                    r = lag * QT + t
                    dp = block[t * TILE:(t + 1) * TILE] - delta
                    dst[r, :, lanes] = dp.astype(BF) * pt[r, :, lanes]
            dq = None
            for lag in range(W):
                ds = dst[lag * QT:(lag + 1) * QT, :, lanes].reshape(QT * TILE, QB)
                here = mm(kt[base + lag], ds)
                dq = here if dq is None else dq + here
            outb[i, fr, 1, 2 * h:2 * h + 2] = (dq * SCALE).astype(BF).T.reshape(2, TILE, HD)

        rows = qg[i, fr, 0].reshape(QT * TILE, HD)
        for lag in range(W):
            block = dst[lag * QT:(lag + 1) * QT].reshape(QT * TILE, QT * TILE)
            acc[i, base + lag, 0] += (mm(block, rows) * SCALE).reshape(QT, TILE, HD)
            block = pt[lag * QT:(lag + 1) * QT].reshape(QT * TILE, QT * TILE)
            acc[i, base + lag, 1] += mm(block, gs[...]).reshape(QT, TILE, HD)

    def back(job):
        @pl.when(has_prev[job])
        def _():
            for s in range(2):
                for a in range(2):
                    g_out[job, s, a] = acc[job, 4 - 2 * job + s, a].astype(BF)
                    send(g_out.at[job, s, a], g_in.at[job, s, a], g_send.at[job, s, a],
                         g_recv.at[job, s, a], prv[job])

    def finish(job):
        for s in range(2):
            for a in range(2):
                @pl.when(has_next[job])
                def _():
                    wait_for(g_in.at[job, s, a], g_recv.at[job, s, a])

                fr = 3 - 2 * job - s
                outb[job, fr, 2 + a] = (acc[job, s, a] + g_in[job, s, a].astype(F32)).astype(BF)
                leave(job, fr, 2 + a)

    units = 6 - 2 * core

    @pl.loop(0, units)
    def _(u):
        job = u // 4
        fr = u - 4 * job
        base = 3 - 2 * job - fr
        wait_for(qg.at[job, fr], qg_in.at[job, fr])

        def arrived(at):
            @pl.when(has_prev[at])
            def _():
                for s in range(2):
                    wait_for(kv.at[at, 4 - 2 * at + s], next_in.at[at, s])

        @pl.when((u == 0) | (u == 4))
        def _():
            each_job(job, arrived)

        attend(job, fr, base, fr + 2 * pair * job, (u == 0) | (u == 4))
        leave(job, fr, 0)
        leave(job, fr, 1)

        @pl.when((u == 1) & (core == 0))
        def _():
            own(1)

        @pl.when((u == 1) | (u == 5))
        def _():
            each_job(job, back)

        @pl.when((u == 2) | (u == 3))
        def _():
            for a in range(2):
                outb[0, u - 2, 2 + a] = acc[0, 5 - u, a].astype(BF)
                leave(0, u - 2, 2 + a)

        @pl.when(u == 3)
        def _():
            finish(0)

    @pl.when(core == 0)
    def _():
        finish(1)

    for at in range(QT):
        for dx in range(4):
            if dx:
                wait_for(qg.at[0, 0, 0], full_send.at[dx, at])
            else:
                @pl.when(at != seat)
                def _():
                    wait_for(qg.at[0, 0, 0], full_send.at[dx, at])

    for e in range(4):
        other, at = half_at(e, pair)

        @pl.when(jnp.logical_not((other == x) & (at == seat)))
        def _():
            wait_for(qg.at[0, 0, 0], half_send.at[e])

    @pl.loop(0, 2 - core)
    def _(job):
        @pl.loop(0, 4 - 2 * job)
        def _(fr):
            for a in range(4):
                for dj in range(QT):
                    if dj:
                        wait_for(outb.at[job, fr, a, dj], out_send.at[job, fr, a, dj])
                    else:
                        @pl.when(fr + 2 * pair * job != x)
                        def _():
                            wait_for(outb.at[job, fr, a, dj], out_send.at[job, fr, a, dj])

    def sent(job):
        for s in range(2):
            @pl.when(has_next[job])
            def _():
                wait_for(kv.at[job, s], next_send.at[job, s])

            @pl.when(has_prev[job])
            def _():
                for a in range(2):
                    wait_for(g_out.at[job, s, a], g_send.at[job, s, a])

    sent(0)

    @pl.when(core == 0)
    def _():
        sent(1)

    for a, ref in enumerate((o_ref, dq_ref, dk_ref, dv_ref)):
        wait_for(ref, out_recv.at[a])


def put(*refs):
    sems = refs[8]
    copies = [pltpu.make_async_copy(refs[a], refs[4 + a], sems.at[a]) for a in range(4)]
    for copy in copies:
        copy.start()
    for copy in copies:
        copy.wait()


def shards(n, query, keys, values, grad_out, tile_pattern, window):
    rows, width = query.shape
    blocks = (QT, TILE, HD)
    dma = pltpu.SemaphoreType.DMA
    scratch = [
        pltpu.VMEM((2, 4, 2) + blocks, BF),
        pltpu.VMEM((2, 6, 2) + blocks, BF),
        pltpu.VMEM((4, QH, W * QT, 1, QB), F32),
        pltpu.VMEM((6, HD, QT * TILE), BF),
        pltpu.VMEM((6, HD, QT * TILE), BF),
        pltpu.VMEM((QH, W * QT, TILE, QB), F32),
        pltpu.VMEM((W * QT, TILE, QT * TILE), BF),
        pltpu.VMEM((W * QT, TILE, QT * TILE), BF),
        pltpu.VMEM((QT * TILE, HD), BF),
        pltpu.VMEM((2, 6, 2) + blocks, F32),
        pltpu.VMEM((2, 2, 2) + blocks, BF),
        pltpu.VMEM((2, 2, 2) + blocks, BF),
        pltpu.VMEM((2, 4, 4) + blocks, BF),
        dma((4, QT)), dma((4,)), dma((2, 4)), dma((2, 4)),
        dma((2, 2)), dma((2, 2)),
        dma((2, 2, 2)), dma((2, 2, 2)),
        dma((2, 4, 4, QT)), dma((4,)),
    ]
    smem = pl.BlockSpec(memory_space=pltpu.SMEM)
    anywhere = pl.BlockSpec(memory_space=pl.ANY)
    held = pl.pallas_call(
        functools.partial(kernel, n),
        out_shape=[pltpu.VMEM((rows, width), BF)] * 4,
        in_specs=[smem, smem] + [anywhere] * 4,
        out_specs=[pl.BlockSpec(memory_space=pltpu.VMEM)] * 4,
        scratch_shapes=scratch,
        compiler_params=pltpu.CompilerParams(
            collective_id=0, has_side_effects=True, vmem_limit_bytes=56 * 1024 * 1024
        ),
    )(tile_pattern, window, query, keys, values, grad_out)
    return pl.pallas_call(
        put,
        out_shape=[jax.ShapeDtypeStruct((rows, width), BF)] * 4,
        in_specs=[pl.BlockSpec(memory_space=pltpu.VMEM)] * 4,
        out_specs=[anywhere] * 4,
        scratch_shapes=[dma((4,))],
    )(*[pltpu.with_memory_space_constraint(part, pltpu.VMEM) for part in held])


def solution(mesh):
    rows = P(("tm", "head"), None)
    return jax.shard_map(
        functools.partial(shards, mesh.shape["tm"]),
        mesh=mesh,
        in_specs=(rows, rows, rows, rows, P(), P()),
        out_specs=(rows, rows, rows, rows),
        check_vma=False,
    )
```

```python
import functools
import math

import jax
import jax.numpy as jnp
from jax import lax
from jax.experimental import pallas as pl
from jax.experimental.pallas import tpu as pltpu
from jax.sharding import PartitionSpec as P

HD = 128
TILE = 128
QT = 4
SEL = 3
W = 3
QH = 2
QB = QT // QH * TILE
NEG = -1e30
SCALE = 1.0 / math.sqrt(HD)
FACTOR = SCALE / math.log(2.0)
MESH = pl.DeviceIdType.MESH
BF = jnp.bfloat16
F32 = jnp.float32


def kernel(
    n,
    pat_any, win_any, q_ref, k_ref, v_ref, g_ref,
    o_ref, dq_ref, dk_ref, dv_ref,
    qg, kv, bias, kt, vt, score, pt, dst, gs, acc, g_out, g_in, outb,
    full_send, half_send, kv_in, qg_in, next_send, next_in, g_send, g_recv, out_send, out_recv,
    pat_ref, win_ref, table_in,
):
    f = lax.axis_index("tm")
    seat = lax.axis_index("head")
    half = n // 2
    rows = n // 4
    row, x = f // 4, lax.rem(f, 4)
    pair, core = x // 2, lax.rem(seat, 2)
    upper = f // half
    full_heads = 4 * QT

    def column_of(at):
        return lax.rem(at // 2 + upper, 2)

    def full_head(other, at):
        return other * 4 + column_of(at) * 2 + lax.rem(at, 2)

    def half_at(e, p):
        return e % 2 + p * (3 - 2 * (e % 2)), 2 * lax.rem(e // 2 + upper, 2)

    my_head = (full_head(x, seat), full_heads + lax.rem(x + pair, 2) + 2 * column_of(seat))

    def device(frame):
        turn = (frame + n) // half - (f + n) // half
        return (frame, lax.rem(seat + 2 * turn + 2 * QT, QT))

    nxt = (device(f + 4), device(4 * (row + pair) + 3 - x))
    prv = (device(f - 4), device(4 * (row + pair - 1) + 3 - x))
    has_next = (row < rows - 1, 2 * row + pair < 2 * rows - 1)
    has_prev = (row > 0, 2 * row + pair > 0)

    def each_job(job, action):
        for at in range(2):
            @pl.when(job == at)
            def _():
                action(at)

    tables = [pltpu.make_async_copy(pat_any, pat_ref, table_in.at[0]),
              pltpu.make_async_copy(win_any, win_ref, table_in.at[1])]
    for table in tables:
        table.start()

    barrier = pltpu.get_barrier_semaphore()

    def greet(who):
        pl.semaphore_signal(barrier, inc=1, device_id=who, device_id_type=MESH)

    for dx in range(4):
        for dj in range(QT):
            if dx or dj:
                greet((4 * row + lax.rem(x + dx, 4), lax.rem(seat + dj, QT)))

    @pl.when(has_next[0])
    def _():
        greet(nxt[0])

    @pl.when(has_prev[0])
    def _():
        greet(prv[0])

    @pl.when((pair == 1) & has_next[0])
    def _():
        greet(nxt[1])

    @pl.when((pair == 0) & has_prev[0])
    def _():
        greet(prv[1])

    not_first = (row + rows - 1) // rows
    not_last = (2 * rows - 2 - row) // rows
    pl.semaphore_wait(barrier, 15 + (2 - pair) * not_first + (1 + pair) * not_last)

    def columns(head):
        return pl.ds(pl.multiple_of(head * HD, HD), HD)

    def wait_for(ref, sem):
        pltpu.make_async_copy(ref, ref, sem).wait()

    def send(src, dst, ssem, rsem, device):
        pltpu.make_async_remote_copy(
            src_ref=src, dst_ref=dst, send_sem=ssem, recv_sem=rsem,
            device_id=device, device_id_type=MESH,
        ).start()

    def place(refs, head, slot, ssem, rsem, other, at, local):
        cols = columns(head)
        if local is not False:
            @pl.when(local)
            def _():
                for a, ref in enumerate(refs):
                    pltpu.make_async_copy(ref.at[:, cols], slot.at[a, seat], rsem).start()

        @pl.when(True if local is False else jnp.logical_not(local))
        def _():
            for a, ref in enumerate(refs):
                send(ref.at[:, cols], slot.at[a, seat], ssem, rsem, (4 * row + other, at))

    side = lax.rem(x, 2)

    def enter_full(refs, slot, rsem, parity):
        for dx in (2, 1, 3, 0):
            for at in (parity, parity + 2):
                other = lax.rem(x + dx, 4)
                place(refs, full_head(other, at), slot, full_send.at[dx, at], rsem,
                      other, at, False if dx else seat == at)

    def enter_half(refs, slot, rsem):
        for e in range(4):
            other, at = half_at(e, pair)
            place(refs, full_heads + e, slot, half_send.at[e], rsem,
                  other, at, (other == x) & (at == seat))

    keys, tops = (k_ref, v_ref), (q_ref, g_ref)

    def full_kv(parity):
        enter_full(keys, kv.at[0, 3 - x], kv_in.at[0, 3 - x], parity)

    def full_qg(parity):
        enter_full(tops, qg.at[0, x], qg_in.at[0, x], parity)

    def own(job):
        for s in range(4 - 2 * job):
            wait_for(kv.at[job, s], kv_in.at[job, s])
            if s < 2:
                @pl.when(has_next[job])
                def _():
                    send(kv.at[job, s], kv.at[job, 4 - 2 * job + s],
                         next_send.at[job, s], next_in.at[job, s], nxt[job])

    full_kv(0)
    full_qg(0)
    enter_half(keys, kv.at[1, 1 - side], kv_in.at[1, 1 - side])

    lane = lax.broadcasted_iota(jnp.int32, (1, QB), 1)
    for table in tables:
        table.wait()

    @pl.loop(0, 4)
    def _(fx):
        frame = 4 * row + fx
        limit = win_ref[frame]
        for h in range(QH):
            for lag in range(W):
                for t in range(QT):
                    both = []
                    for tile in (2 * h, 2 * h + 1):
                        hit = pat_ref[lag, tile, 0] == t
                        for s in range(1, SEL):
                            hit = hit | (pat_ref[lag, tile, s] == t)
                        hit = hit & (lag <= frame) & (lag < limit)
                        both.append(jnp.where(hit, 0.0, NEG).astype(F32))
                    bias[fx, h, lag * QT + t] = jnp.where(lane < TILE, both[0], both[1])

    full_kv(1)

    @pl.loop(0, 2)
    def _(job):
        @pl.loop(0, 6)
        def _(s):
            acc[job, s] = jnp.zeros(acc.shape[2:], F32)

    for job in range(2):
        for s in range(2):
            @pl.when(jnp.logical_not(has_prev[job]))
            def _():
                kv[job, 4 - 2 * job + s] = jnp.zeros(kv.shape[2:], BF)

            @pl.when(jnp.logical_not(has_next[job]))
            def _():
                g_in[job, s] = jnp.zeros(g_in.shape[2:], BF)

    @pl.when(core == 0)
    def _():
        own(0)

    full_qg(1)
    enter_half(tops, qg.at[1, side], qg_in.at[1, side])

    @pl.when(core == 1)
    def _():
        own(0)

    def leave(job, fr, a):
        ref = (o_ref, dq_ref, dk_ref, dv_ref)[a]
        where_to = ref.at[:, columns(jnp.where(job == 0, my_head[0], my_head[1]))]
        owner = fr + 2 * pair * job
        for dj in range(QT):
            at = lax.rem(seat + dj, QT)
            src = outb.at[job, fr, a, at]
            if dj:
                send(src, where_to, out_send.at[job, fr, a, dj], out_recv.at[a], (4 * row + owner, at))
            else:
                @pl.when(owner == x)
                def _():
                    pltpu.make_async_copy(src, where_to, out_recv.at[a]).start()

                @pl.when(owner != x)
                def _():
                    send(src, where_to, out_send.at[job, fr, a, dj], out_recv.at[a], (4 * row + owner, at))

    def nt(a, b):
        return lax.dot_general(a, b, (((1,), (1,)), ((), ())), preferred_element_type=F32)

    def mm(a, b):
        return jnp.dot(a, b, preferred_element_type=F32)

    def fold(block, op):
        return op(block.reshape(TILE // 8, 8, QB), axis=0)

    def attend(i, fr, base, x, first):

        def turn(slot):
            kt[slot] = kv[i, slot, 0].reshape(QT * TILE, HD).T
            vt[slot] = kv[i, slot, 1].reshape(QT * TILE, HD).T

        turn(base)

        @pl.when(first)
        def _():
            turn(base + 1)
            turn(base + 2)

        for h in range(QH):
            lanes = slice(h * QB, (h + 1) * QB)
            qh = qg[i, fr, 0, 2 * h:2 * h + 2].reshape(QB, HD)
            gh = qg[i, fr, 1, 2 * h:2 * h + 2].reshape(QB, HD)
            top = None
            for lag in range(W):
                block = nt(kv[i, base + lag, 0].reshape(QT * TILE, HD), qh)
                for t in range(QT):
                    r = lag * QT + t
                    s = block[t * TILE:(t + 1) * TILE]
                    score[h, r] = s
                    here = fold(s, jnp.max) + bias[x, h, r]
                    top = here if top is None else jnp.maximum(top, here)
            top = jnp.max(top, axis=0, keepdims=True)
            total = None
            for r in range(W * QT):
                e = jnp.exp2(score[h, r] * FACTOR + (bias[x, h, r] - top) * FACTOR)
                pt[r, :, lanes] = e.astype(BF)
                here = fold(e, jnp.sum)
                total = here if total is None else total + here
            inverse = 1.0 / jnp.sum(total, axis=0, keepdims=True)
            out = None
            for lag in range(W):
                probs = pt[lag * QT:(lag + 1) * QT, :, lanes].reshape(QT * TILE, QB)
                here = mm(vt[base + lag], probs)
                out = here if out is None else out + here
            out = out * inverse
            scaled = (gh.T.astype(F32) * inverse).astype(BF)
            delta = jnp.sum(scaled.astype(F32) * out, axis=0, keepdims=True)
            outb[i, fr, 0, 2 * h:2 * h + 2] = out.astype(BF).T.reshape(2, TILE, HD)
            back = scaled.T
            gs[lanes] = back
            for lag in range(W):
                block = nt(kv[i, base + lag, 1].reshape(QT * TILE, HD), back)
                for t in range(QT):
                    r = lag * QT + t
                    dp = block[t * TILE:(t + 1) * TILE] - delta
                    dst[r, :, lanes] = dp.astype(BF) * pt[r, :, lanes]
            dq = None
            for lag in range(W):
                ds = dst[lag * QT:(lag + 1) * QT, :, lanes].reshape(QT * TILE, QB)
                here = mm(kt[base + lag], ds)
                dq = here if dq is None else dq + here
            outb[i, fr, 1, 2 * h:2 * h + 2] = (dq * SCALE).astype(BF).T.reshape(2, TILE, HD)

        rows = qg[i, fr, 0].reshape(QT * TILE, HD)
        for lag in range(W):
            block = dst[lag * QT:(lag + 1) * QT].reshape(QT * TILE, QT * TILE)
            acc[i, base + lag, 0] += (mm(block, rows) * SCALE).reshape(QT, TILE, HD)
            block = pt[lag * QT:(lag + 1) * QT].reshape(QT * TILE, QT * TILE)
            acc[i, base + lag, 1] += mm(block, gs[...]).reshape(QT, TILE, HD)

    def back(job):
        @pl.when(has_prev[job])
        def _():
            for s in range(2):
                for a in range(2):
                    g_out[job, s, a] = acc[job, 4 - 2 * job + s, a].astype(BF)
                    send(g_out.at[job, s, a], g_in.at[job, s, a], g_send.at[job, s, a],
                         g_recv.at[job, s, a], prv[job])

    def finish(job):
        for s in range(2):
            for a in range(2):
                @pl.when(has_next[job])
                def _():
                    wait_for(g_in.at[job, s, a], g_recv.at[job, s, a])

                fr = 3 - 2 * job - s
                outb[job, fr, 2 + a] = (acc[job, s, a] + g_in[job, s, a].astype(F32)).astype(BF)
                leave(job, fr, 2 + a)

    units = 6 - 2 * core

    @pl.loop(0, units)
    def _(u):
        job = u // 4
        fr = u - 4 * job
        base = 3 - 2 * job - fr
        wait_for(qg.at[job, fr], qg_in.at[job, fr])

        def arrived(at):
            @pl.when(has_prev[at])
            def _():
                for s in range(2):
                    wait_for(kv.at[at, 4 - 2 * at + s], next_in.at[at, s])

        @pl.when((u == 0) | (u == 4))
        def _():
            each_job(job, arrived)

        attend(job, fr, base, fr + 2 * pair * job, (u == 0) | (u == 4))
        leave(job, fr, 0)
        leave(job, fr, 1)

        @pl.when((u == 0) & (core == 0))
        def _():
            own(1)

        @pl.when((u == 1) | (u == 5))
        def _():
            each_job(job, back)

        @pl.when((u == 2) | (u == 3))
        def _():
            for a in range(2):
                outb[0, u - 2, 2 + a] = acc[0, 5 - u, a].astype(BF)
                leave(0, u - 2, 2 + a)

        @pl.when(u == 3)
        def _():
            finish(0)

    @pl.when(core == 0)
    def _():
        finish(1)

    for at in range(QT):
        for dx in range(4):
            if dx:
                wait_for(qg.at[0, 0, 0], full_send.at[dx, at])
            else:
                @pl.when(at != seat)
                def _():
                    wait_for(qg.at[0, 0, 0], full_send.at[dx, at])

    for e in range(4):
        other, at = half_at(e, pair)

        @pl.when(jnp.logical_not((other == x) & (at == seat)))
        def _():
            wait_for(qg.at[0, 0, 0], half_send.at[e])

    @pl.loop(0, 2 - core)
    def _(job):
        @pl.loop(0, 4 - 2 * job)
        def _(fr):
            for a in range(4):
                for dj in range(QT):
                    if dj:
                        wait_for(outb.at[job, fr, a, dj], out_send.at[job, fr, a, dj])
                    else:
                        @pl.when(fr + 2 * pair * job != x)
                        def _():
                            wait_for(outb.at[job, fr, a, dj], out_send.at[job, fr, a, dj])

    def sent(job):
        for s in range(2):
            @pl.when(has_next[job])
            def _():
                wait_for(kv.at[job, s], next_send.at[job, s])

            @pl.when(has_prev[job])
            def _():
                for a in range(2):
                    wait_for(g_out.at[job, s, a], g_send.at[job, s, a])

    sent(0)

    @pl.when(core == 0)
    def _():
        sent(1)

    for a, ref in enumerate((o_ref, dq_ref, dk_ref, dv_ref)):
        wait_for(ref, out_recv.at[a])


def put(*refs):
    sems = refs[8]
    copies = [pltpu.make_async_copy(refs[a], refs[4 + a], sems.at[a]) for a in range(4)]
    for copy in copies:
        copy.start()
    for copy in copies:
        copy.wait()


def shards(n, query, keys, values, grad_out, tile_pattern, window):
    rows, width = query.shape
    blocks = (QT, TILE, HD)
    dma = pltpu.SemaphoreType.DMA
    scratch = [
        pltpu.VMEM((2, 4, 2) + blocks, BF),
        pltpu.VMEM((2, 6, 2) + blocks, BF),
        pltpu.VMEM((4, QH, W * QT, 1, QB), F32),
        pltpu.VMEM((6, HD, QT * TILE), BF),
        pltpu.VMEM((6, HD, QT * TILE), BF),
        pltpu.VMEM((QH, W * QT, TILE, QB), F32),
        pltpu.VMEM((W * QT, TILE, QT * TILE), BF),
        pltpu.VMEM((W * QT, TILE, QT * TILE), BF),
        pltpu.VMEM((QT * TILE, HD), BF),
        pltpu.VMEM((2, 6, 2) + blocks, F32),
        pltpu.VMEM((2, 2, 2) + blocks, BF),
        pltpu.VMEM((2, 2, 2) + blocks, BF),
        pltpu.VMEM((2, 4, 4) + blocks, BF),
        dma((4, QT)), dma((4,)), dma((2, 4)), dma((2, 4)),
        dma((2, 2)), dma((2, 2)),
        dma((2, 2, 2)), dma((2, 2, 2)),
        dma((2, 4, 4, QT)), dma((4,)),
        pltpu.SMEM(tile_pattern.shape, jnp.int32), pltpu.SMEM(window.shape, jnp.int32), dma((2,)),
    ]
    anywhere = pl.BlockSpec(memory_space=pl.ANY)
    held = pl.pallas_call(
        functools.partial(kernel, n),
        out_shape=[pltpu.VMEM((rows, width), BF)] * 4,
        in_specs=[anywhere] * 6,
        out_specs=[pl.BlockSpec(memory_space=pltpu.VMEM)] * 4,
        scratch_shapes=scratch,
        compiler_params=pltpu.CompilerParams(
            collective_id=0, has_side_effects=True, vmem_limit_bytes=56 * 1024 * 1024
        ),
    )(tile_pattern, window, query, keys, values, grad_out)
    return pl.pallas_call(
        put,
        out_shape=[jax.ShapeDtypeStruct((rows, width), BF)] * 4,
        in_specs=[pl.BlockSpec(memory_space=pltpu.VMEM)] * 4,
        out_specs=[anywhere] * 4,
        scratch_shapes=[dma((4,))],
    )(*[pltpu.with_memory_space_constraint(part, pltpu.VMEM) for part in held])


def solution(mesh):
    rows = P(("tm", "head"), None)
    return jax.shard_map(
        functools.partial(shards, mesh.shape["tm"]),
        mesh=mesh,
        in_specs=(rows, rows, rows, rows, P(), P()),
        out_specs=(rows, rows, rows, rows),
        check_vma=False,
    )
```

```python
import functools
import math

import jax
import jax.numpy as jnp
from jax import lax
from jax.experimental import pallas as pl
from jax.experimental.pallas import tpu as pltpu
from jax.sharding import PartitionSpec as P

HD = 128
TILE = 128
QT = 4
SEL = 3
W = 3
QH = 2
QB = QT // QH * TILE
NEG = -1e30
SCALE = 1.0 / math.sqrt(HD)
FACTOR = SCALE / math.log(2.0)
MESH = pl.DeviceIdType.MESH
BF = jnp.bfloat16
F32 = jnp.float32


def kernel(
    n,
    pat_any, win_any, q_ref, k_ref, v_ref, g_ref,
    o_ref, dq_ref, dk_ref, dv_ref,
    qg, kv, bias, kt, vt, score, pt, dst, gs, acc, g_out, g_in, outb,
    full_send, half_send, kv_in, qg_in, next_send, next_in, g_send, g_recv, out_send, out_recv,
    pat_ref, win_ref, table_in,
):
    f = lax.axis_index("tm")
    seat = lax.axis_index("head")
    half = n // 2
    rows = n // 4
    row, x = f // 4, lax.rem(f, 4)
    pair, core = x // 2, lax.rem(seat, 2)
    upper = f // half
    full_heads = 4 * QT

    def column_of(at):
        return lax.rem(at // 2 + upper, 2)

    def full_head(other, at):
        return other * 4 + column_of(at) * 2 + lax.rem(at, 2)

    def half_at(e, p):
        return e % 2 + p * (3 - 2 * (e % 2)), 2 * lax.rem(e // 2 + upper, 2)

    my_head = (full_head(x, seat), full_heads + lax.rem(x + pair, 2) + 2 * column_of(seat))

    def device(frame):
        turn = (frame + n) // half - (f + n) // half
        return (frame, lax.rem(seat + 2 * turn + 2 * QT, QT))

    nxt = (device(f + 4), device(4 * (row + pair) + 3 - x))
    prv = (device(f - 4), device(4 * (row + pair - 1) + 3 - x))
    has_next = (row < rows - 1, 2 * row + pair < 2 * rows - 1)
    has_prev = (row > 0, 2 * row + pair > 0)

    def each_job(job, action):
        for at in range(2):
            @pl.when(job == at)
            def _():
                action(at)

    tables = [pltpu.make_async_copy(pat_any, pat_ref, table_in.at[0]),
              pltpu.make_async_copy(win_any, win_ref, table_in.at[1])]
    for table in tables:
        table.start()

    barrier = pltpu.get_barrier_semaphore()

    def greet(who):
        pl.semaphore_signal(barrier, inc=1, device_id=who, device_id_type=MESH)

    for dx in range(4):
        for dj in range(QT):
            if dx or dj:
                greet((4 * row + lax.rem(x + dx, 4), lax.rem(seat + dj, QT)))

    @pl.when(has_next[0])
    def _():
        greet(nxt[0])

    @pl.when(has_prev[0])
    def _():
        greet(prv[0])

    @pl.when((pair == 1) & has_next[0])
    def _():
        greet(nxt[1])

    @pl.when((pair == 0) & has_prev[0])
    def _():
        greet(prv[1])

    not_first = (row + rows - 1) // rows
    not_last = (2 * rows - 2 - row) // rows
    pl.semaphore_wait(barrier, 15 + (2 - pair) * not_first + (1 + pair) * not_last)

    def columns(head):
        return pl.ds(pl.multiple_of(head * HD, HD), HD)

    def wait_for(ref, sem):
        pltpu.make_async_copy(ref, ref, sem).wait()

    def send(src, dst, ssem, rsem, device):
        pltpu.make_async_remote_copy(
            src_ref=src, dst_ref=dst, send_sem=ssem, recv_sem=rsem,
            device_id=device, device_id_type=MESH,
        ).start()

    def place(refs, head, slot, ssem, rsem, other, at, local):
        cols = columns(head)
        if local is not False:
            @pl.when(local)
            def _():
                for a, ref in enumerate(refs):
                    pltpu.make_async_copy(ref.at[:, cols], slot.at[a, seat], rsem).start()

        @pl.when(True if local is False else jnp.logical_not(local))
        def _():
            for a, ref in enumerate(refs):
                send(ref.at[:, cols], slot.at[a, seat], ssem, rsem, (4 * row + other, at))

    side = lax.rem(x, 2)

    def enter_full(refs, slot, rsem, parity):
        for dx in (2, 1, 3, 0):
            for at in (parity, parity + 2):
                other = lax.rem(x + dx, 4)
                place(refs, full_head(other, at), slot, full_send.at[dx, at], rsem,
                      other, at, False if dx else seat == at)

    def enter_half(refs, slot, rsem):
        for e in range(4):
            other, at = half_at(e, pair)
            place(refs, full_heads + e, slot, half_send.at[e], rsem,
                  other, at, (other == x) & (at == seat))

    keys, tops = (k_ref, v_ref), (q_ref, g_ref)

    def full_kv(parity):
        enter_full(keys, kv.at[0, 3 - x], kv_in.at[0, 3 - x], parity)

    def full_qg(parity):
        enter_full(tops, qg.at[0, x], qg_in.at[0, x], parity)

    def own(job):
        for s in range(4 - 2 * job):
            wait_for(kv.at[job, s], kv_in.at[job, s])
            if s < 2:
                @pl.when(has_next[job])
                def _():
                    send(kv.at[job, s], kv.at[job, 4 - 2 * job + s],
                         next_send.at[job, s], next_in.at[job, s], nxt[job])

    full_kv(0)
    full_qg(0)
    enter_half(keys, kv.at[1, 1 - side], kv_in.at[1, 1 - side])

    lane = lax.broadcasted_iota(jnp.int32, (1, QB), 1)
    for table in tables:
        table.wait()

    @pl.loop(0, 4)
    def _(fx):
        frame = 4 * row + fx
        limit = win_ref[frame]
        for h in range(QH):
            for lag in range(W):
                for t in range(QT):
                    both = []
                    for tile in (2 * h, 2 * h + 1):
                        hit = pat_ref[lag, tile, 0] == t
                        for s in range(1, SEL):
                            hit = hit | (pat_ref[lag, tile, s] == t)
                        hit = hit & (lag <= frame) & (lag < limit)
                        both.append(jnp.where(hit, 0.0, NEG).astype(F32))
                    bias[fx, h, lag * QT + t] = jnp.where(lane < TILE, both[0], both[1])

    full_kv(1)

    @pl.loop(0, 2)
    def _(job):
        @pl.loop(0, 6)
        def _(s):
            acc[job, s] = jnp.zeros(acc.shape[2:], F32)

    for job in range(2):
        for s in range(2):
            @pl.when(jnp.logical_not(has_prev[job]))
            def _():
                kv[job, 4 - 2 * job + s] = jnp.zeros(kv.shape[2:], BF)

            @pl.when(jnp.logical_not(has_next[job]))
            def _():
                g_in[job, s] = jnp.zeros(g_in.shape[2:], BF)

    @pl.when(core == 0)
    def _():
        own(0)

    full_qg(1)
    enter_half(tops, qg.at[1, side], qg_in.at[1, side])

    @pl.when(core == 1)
    def _():
        own(0)

    def leave(job, fr, a):
        ref = (o_ref, dq_ref, dk_ref, dv_ref)[a]
        where_to = ref.at[:, columns(jnp.where(job == 0, my_head[0], my_head[1]))]
        owner = fr + 2 * pair * job
        for dj in range(QT):
            at = lax.rem(seat + dj, QT)
            src = outb.at[job, fr, a, at]
            if dj:
                send(src, where_to, out_send.at[job, fr, a, dj], out_recv.at[a], (4 * row + owner, at))
            else:
                @pl.when(owner == x)
                def _():
                    pltpu.make_async_copy(src, where_to, out_recv.at[a]).start()

                @pl.when(owner != x)
                def _():
                    send(src, where_to, out_send.at[job, fr, a, dj], out_recv.at[a], (4 * row + owner, at))

    def nt(a, b):
        return lax.dot_general(a, b, (((1,), (1,)), ((), ())), preferred_element_type=F32)

    def mm(a, b):
        return jnp.dot(a, b, preferred_element_type=F32)

    def fold(block, op):
        return op(block.reshape(TILE // 8, 8, QB), axis=0)

    def attend(i, fr, base, x, first):

        def turn(slot):
            kt[slot] = kv[i, slot, 0].reshape(QT * TILE, HD).T
            vt[slot] = kv[i, slot, 1].reshape(QT * TILE, HD).T

        turn(base)

        @pl.when(first)
        def _():
            turn(base + 1)
            turn(base + 2)

        for h in range(QH):
            lanes = slice(h * QB, (h + 1) * QB)
            qh = qg[i, fr, 0, 2 * h:2 * h + 2].reshape(QB, HD)
            gh = qg[i, fr, 1, 2 * h:2 * h + 2].reshape(QB, HD)
            top = None
            for lag in range(W):
                block = nt(kv[i, base + lag, 0].reshape(QT * TILE, HD), qh)
                for t in range(QT):
                    r = lag * QT + t
                    s = block[t * TILE:(t + 1) * TILE]
                    score[h, r] = s
                    here = fold(s, jnp.max) + bias[x, h, r]
                    top = here if top is None else jnp.maximum(top, here)
            top = jnp.max(top, axis=0, keepdims=True)
            total = None
            for r in range(W * QT):
                e = jnp.exp2(score[h, r] * FACTOR + (bias[x, h, r] - top) * FACTOR)
                pt[r, :, lanes] = e.astype(BF)
                here = fold(e, jnp.sum)
                total = here if total is None else total + here
            inverse = 1.0 / jnp.sum(total, axis=0, keepdims=True)
            out = None
            for lag in range(W):
                probs = pt[lag * QT:(lag + 1) * QT, :, lanes].reshape(QT * TILE, QB)
                here = mm(vt[base + lag], probs)
                out = here if out is None else out + here
            out = out * inverse
            scaled = (gh.T.astype(F32) * inverse).astype(BF)
            delta = jnp.sum(scaled.astype(F32) * out, axis=0, keepdims=True)
            outb[i, fr, 0, 2 * h:2 * h + 2] = out.astype(BF).T.reshape(2, TILE, HD)
            back = scaled.T
            gs[lanes] = back
            for lag in range(W):
                block = nt(kv[i, base + lag, 1].reshape(QT * TILE, HD), back)
                for t in range(QT):
                    r = lag * QT + t
                    dp = block[t * TILE:(t + 1) * TILE] - delta
                    dst[r, :, lanes] = dp.astype(BF) * pt[r, :, lanes]
            dq = None
            for lag in range(W):
                ds = dst[lag * QT:(lag + 1) * QT, :, lanes].reshape(QT * TILE, QB)
                here = mm(kt[base + lag], ds)
                dq = here if dq is None else dq + here
            outb[i, fr, 1, 2 * h:2 * h + 2] = (dq * SCALE).astype(BF).T.reshape(2, TILE, HD)

        rows = qg[i, fr, 0].reshape(QT * TILE, HD)
        for lag in range(W):
            block = dst[lag * QT:(lag + 1) * QT].reshape(QT * TILE, QT * TILE)
            acc[i, base + lag, 0] += (mm(block, rows) * SCALE).reshape(QT, TILE, HD)
            block = pt[lag * QT:(lag + 1) * QT].reshape(QT * TILE, QT * TILE)
            acc[i, base + lag, 1] += mm(block, gs[...]).reshape(QT, TILE, HD)

    def back(job):
        @pl.when(has_prev[job])
        def _():
            for s in range(2):
                for a in range(2):
                    g_out[job, s, a] = acc[job, 4 - 2 * job + s, a].astype(BF)
                    send(g_out.at[job, s, a], g_in.at[job, s, a], g_send.at[job, s, a],
                         g_recv.at[job, s, a], prv[job])

    def finish(job):
        for s in range(2):
            for a in range(2):
                @pl.when(has_next[job])
                def _():
                    wait_for(g_in.at[job, s, a], g_recv.at[job, s, a])

                fr = 3 - 2 * job - s
                outb[job, fr, 2 + a] = (acc[job, s, a] + g_in[job, s, a].astype(F32)).astype(BF)
                leave(job, fr, 2 + a)

    units = 6 - 2 * core

    @pl.loop(0, units)
    def _(u):
        job = u // 4
        fr = u - 4 * job
        base = 3 - 2 * job - fr
        wait_for(qg.at[job, fr], qg_in.at[job, fr])

        def arrived(at):
            @pl.when(has_prev[at])
            def _():
                for s in range(2):
                    wait_for(kv.at[at, 4 - 2 * at + s], next_in.at[at, s])

        @pl.when((u == 0) | (u == 4))
        def _():
            each_job(job, arrived)

        attend(job, fr, base, fr + 2 * pair * job, (u == 0) | (u == 4))

        @pl.when((u == 1) | (u == 5))
        def _():
            each_job(job, back)

        leave(job, fr, 0)
        leave(job, fr, 1)

        @pl.when((u == 0) & (core == 0))
        def _():
            own(1)

        @pl.when((u == 2) | (u == 3))
        def _():
            for a in range(2):
                outb[0, u - 2, 2 + a] = acc[0, 5 - u, a].astype(BF)
                leave(0, u - 2, 2 + a)

        @pl.when(u == 3)
        def _():
            finish(0)

    @pl.when(core == 0)
    def _():
        finish(1)

    for at in range(QT):
        for dx in range(4):
            if dx:
                wait_for(qg.at[0, 0, 0], full_send.at[dx, at])
            else:
                @pl.when(at != seat)
                def _():
                    wait_for(qg.at[0, 0, 0], full_send.at[dx, at])

    for e in range(4):
        other, at = half_at(e, pair)

        @pl.when(jnp.logical_not((other == x) & (at == seat)))
        def _():
            wait_for(qg.at[0, 0, 0], half_send.at[e])

    @pl.loop(0, 2 - core)
    def _(job):
        @pl.loop(0, 4 - 2 * job)
        def _(fr):
            for a in range(4):
                for dj in range(QT):
                    if dj:
                        wait_for(outb.at[job, fr, a, dj], out_send.at[job, fr, a, dj])
                    else:
                        @pl.when(fr + 2 * pair * job != x)
                        def _():
                            wait_for(outb.at[job, fr, a, dj], out_send.at[job, fr, a, dj])

    def sent(job):
        for s in range(2):
            @pl.when(has_next[job])
            def _():
                wait_for(kv.at[job, s], next_send.at[job, s])

            @pl.when(has_prev[job])
            def _():
                for a in range(2):
                    wait_for(g_out.at[job, s, a], g_send.at[job, s, a])

    sent(0)

    @pl.when(core == 0)
    def _():
        sent(1)

    for a, ref in enumerate((o_ref, dq_ref, dk_ref, dv_ref)):
        wait_for(ref, out_recv.at[a])


def put(*refs):
    sems = refs[8]
    copies = [pltpu.make_async_copy(refs[a], refs[4 + a], sems.at[a]) for a in range(4)]
    for copy in copies:
        copy.start()
    for copy in copies:
        copy.wait()


def shards(n, query, keys, values, grad_out, tile_pattern, window):
    rows, width = query.shape
    blocks = (QT, TILE, HD)
    dma = pltpu.SemaphoreType.DMA
    scratch = [
        pltpu.VMEM((2, 4, 2) + blocks, BF),
        pltpu.VMEM((2, 6, 2) + blocks, BF),
        pltpu.VMEM((4, QH, W * QT, 1, QB), F32),
        pltpu.VMEM((6, HD, QT * TILE), BF),
        pltpu.VMEM((6, HD, QT * TILE), BF),
        pltpu.VMEM((QH, W * QT, TILE, QB), F32),
        pltpu.VMEM((W * QT, TILE, QT * TILE), BF),
        pltpu.VMEM((W * QT, TILE, QT * TILE), BF),
        pltpu.VMEM((QT * TILE, HD), BF),
        pltpu.VMEM((2, 6, 2) + blocks, F32),
        pltpu.VMEM((2, 2, 2) + blocks, BF),
        pltpu.VMEM((2, 2, 2) + blocks, BF),
        pltpu.VMEM((2, 4, 4) + blocks, BF),
        dma((4, QT)), dma((4,)), dma((2, 4)), dma((2, 4)),
        dma((2, 2)), dma((2, 2)),
        dma((2, 2, 2)), dma((2, 2, 2)),
        dma((2, 4, 4, QT)), dma((4,)),
        pltpu.SMEM(tile_pattern.shape, jnp.int32), pltpu.SMEM(window.shape, jnp.int32), dma((2,)),
    ]
    anywhere = pl.BlockSpec(memory_space=pl.ANY)
    held = pl.pallas_call(
        functools.partial(kernel, n),
        out_shape=[pltpu.VMEM((rows, width), BF)] * 4,
        in_specs=[anywhere] * 6,
        out_specs=[pl.BlockSpec(memory_space=pltpu.VMEM)] * 4,
        scratch_shapes=scratch,
        compiler_params=pltpu.CompilerParams(
            collective_id=0, has_side_effects=True, vmem_limit_bytes=56 * 1024 * 1024
        ),
    )(tile_pattern, window, query, keys, values, grad_out)
    return pl.pallas_call(
        put,
        out_shape=[jax.ShapeDtypeStruct((rows, width), BF)] * 4,
        in_specs=[pl.BlockSpec(memory_space=pltpu.VMEM)] * 4,
        out_specs=[anywhere] * 4,
        scratch_shapes=[dma((4,))],
    )(*[pltpu.with_memory_space_constraint(part, pltpu.VMEM) for part in held])


def solution(mesh):
    rows = P(("tm", "head"), None)
    return jax.shard_map(
        functools.partial(shards, mesh.shape["tm"]),
        mesh=mesh,
        in_specs=(rows, rows, rows, rows, P(), P()),
        out_specs=(rows, rows, rows, rows),
        check_vma=False,
    )
```
